256 devices in a mesh: section: 8 (over z), seq: 8 (over y, core), tp: 4 (over x).
Axes of the slice: x: 4, y: 4, z: 8, core: 2. Of those that a mesh axis runs over, the one named last changes fastest.
Arguments:
- text_rows: bfloat16 [128, 8192], P(None, ('seq', 'tp')), may hold values from -6 to 6
- image_rows: bfloat16 [128, 8192], P(('seq', 'tp')), may hold values from -6 to 6
- image_target: int32 [128], P(('seq', 'tp')), may hold values from -1 to 63, as said below
- norm_gain: bfloat16 [8, 8192], P('section', ('seq', 'tp')), may hold values from 0.099609375 to 1.8984375
- q_weight: bfloat16 [8, 8192, 4096], P('section', None, ('seq', 'tp')), may hold values from -0.0625 to 0.0625
- q_bias: bfloat16 [8, 4096], P('section', ('seq', 'tp')), may hold values from -3 to 3
- kv_weight: bfloat16 [8, 8192, 4, 256], P('section', None, 'tp'), may hold values from -0.0625 to 0.0625
- kv_bias: bfloat16 [8, 4, 256], P('section', 'tp'), may hold values from -3 to 3
- out_weight: bfloat16 [8, 4096, 8192], P('section', None, ('seq', 'tp')), may hold values from -0.09375 to 0.09375
Outputs:
- layer_outputs: bfloat16 [8, 128, 8192], P('section', None, ('seq', 'tp'))
The draws below stay inside these ranges and needn't reach their ends.
Inputs may be any that keep to these rules, and one draw needn't show every extreme that they name: `image_target`: in each micro-batch's 64 entries exactly 56 are token positions, all different, and the others are -1.
All inputs are finite; a program needn't handle non-finite values.
Results may differ from the reference program's by a relative error of at most 0.015.
Values may be sent and summed in bfloat16 or wider, within the bound.
No kernel may reach another device: no remote copies, remote signals or barrier semaphores. Data moves between devices by JAX's collectives and lax.ppermute only.
A program may use at most 64 MiB of HBM per device.

```python
import math
import jax
import jax.numpy as jnp
from jax import lax

D = 8192
HD = 128
SEQ_TOK = 64
MICRO = 2
QH = 32
KVH = 4
LAYERS = 8
SLOTS = 64
IMG = 56


def draw_image_target(key, part):

    def draw_micro(micro_key):
        key_order, key_place = jax.random.split(micro_key, 2)
        ranks = jax.random.permutation(key_order, SLOTS).astype(jnp.int32)
        rest = jax.random.permutation(key_place, SEQ_TOK - 1).astype(jnp.int32)
        places = jnp.concatenate([jnp.full((1,), SEQ_TOK - 1, jnp.int32), rest]).astype(jnp.int32)
        chosen = places[jnp.minimum(ranks, SEQ_TOK - 1)]
        return jnp.where(ranks < IMG, chosen, -1).astype(jnp.int32)
    micro_keys = jax.random.split(key, MICRO)
    return jax.vmap(draw_micro)(micro_keys).reshape(MICRO * SLOTS).astype(jnp.int32)


def level_of(own_key, dims, cuts, low, top_value):
    factor_of, own = 1.0, jax.random.fold_in(own_key, 6)
    for axis_at, parts in cuts:
        steps = jnp.exp(jax.random.uniform(jax.random.fold_in(own, axis_at), (parts,), jnp.float32, low / len(cuts), top_value / len(cuts)))
        factor_of = factor_of * jnp.repeat(steps, dims[axis_at] // parts).reshape([-1 if axis == axis_at else 1 for axis in range(len(dims))])
    return factor_of


def noise(stream_key, extent, deviation, reach, pieces=(), kind=jnp.bfloat16):
    values = deviation * jax.random.normal(stream_key, extent, jnp.float32)
    if pieces:
        values = values * level_of(stream_key, extent, pieces, -0.22, 0.18)
    return jnp.clip(values, -reach, reach).astype(kind)


def setup_inputs(seed: int = 0) -> dict:
    arg_keys = jax.random.split(jax.random.key(seed), 10)
    return {
        "text_rows": noise(arg_keys[0], (MICRO * SEQ_TOK, D), 1.0, 6.0, ((1, 32),)),
        "image_rows": noise(arg_keys[1], (MICRO * SLOTS, D), 1.0, 6.0, ((0, 32),)),
        "image_target": draw_image_target(jax.random.fold_in(arg_keys[9], 71), 0),
        "norm_gain": jnp.clip(1.0 + 0.18 * jax.random.normal(arg_keys[3], (LAYERS, D), jnp.float32), 0.099609375, 1.8984375).astype(jnp.bfloat16),
        "q_weight": noise(arg_keys[4], (LAYERS, D, QH * HD), D ** -0.5, 0.0625, ((0, 8), (2, 32))),
        "q_bias": noise(arg_keys[5], (LAYERS, QH * HD), 0.5, 3.0, ((0, 8), (1, 32))),
        "kv_weight": noise(arg_keys[6], (LAYERS, D, KVH, 2 * HD), D ** -0.5, 0.0625, ((0, 8), (2, 4))),
        "kv_bias": noise(arg_keys[7], (LAYERS, KVH, 2 * HD), 0.5, 3.0, ((0, 8), (1, 4))),
        "out_weight": noise(arg_keys[8], (LAYERS, QH * HD, D), (QH * HD) ** -0.5, 0.09375, ((0, 8), (2, 32))),
    }


EPS = 1e-06
THETA = 1000000.0

def rotate(values, cosine, sine_tab):
    half_size = values.shape[-1] // 2
    turned = jnp.concatenate([-values[..., half_size:], values[..., :half_size]], axis=-1)
    return values * cosine + turned * sine_tab

def reference(text_rows, image_rows, image_target, norm_gain, q_weight, q_bias, kv_weight, kv_bias, out_weight):
    slot_grid = image_target.reshape(MICRO, SLOTS)
    positions = jnp.arange(SEQ_TOK, dtype=jnp.int32)
    matched = slot_grid[:, None, :] == positions[None, :, None]
    pictures = image_rows.reshape(MICRO, SLOTS, D).astype(jnp.float32)
    placed = jnp.einsum('mps,msd->mpd', matched.astype(jnp.float32), pictures, precision=lax.Precision.HIGHEST)
    is_image = jnp.any(matched, axis=-1)
    text_grid = text_rows.reshape(MICRO, SEQ_TOK, D).astype(jnp.float32)
    hidden = jnp.where(is_image[..., None], placed, text_grid).astype(jnp.bfloat16)
    half_size = HD // 2
    frequency = THETA ** (-jnp.arange(half_size, dtype=jnp.float32) * 2.0 / HD)
    angles = positions.astype(jnp.float32)[:, None] * frequency[None, :]
    cosine = jnp.concatenate([jnp.cos(angles), jnp.cos(angles)], axis=-1)[:, None, :]
    sine_tab = jnp.concatenate([jnp.sin(angles), jnp.sin(angles)], axis=-1)[:, None, :]
    causal = positions[:, None] >= positions[None, :]
    head_group = jnp.arange(QH) % KVH
    collected = []
    for layer in range(LAYERS):
        residual = hidden.reshape(MICRO * SEQ_TOK, D).astype(jnp.float32)
        inv_rms = lax.rsqrt(lax.optimization_barrier(jnp.mean(residual * residual, axis=-1, keepdims=True)) + EPS)
        normed = (residual * inv_rms * norm_gain[layer].astype(jnp.float32)).astype(jnp.bfloat16)
        queries = jnp.dot(normed, q_weight[layer], preferred_element_type=jnp.float32) + q_bias[layer].astype(jnp.float32)
        keyval = jnp.dot(normed, kv_weight[layer].reshape(D, KVH * 2 * HD), preferred_element_type=jnp.float32)
        keyval = keyval + kv_bias[layer].reshape(KVH * 2 * HD).astype(jnp.float32)
        queries = queries.reshape(MICRO, SEQ_TOK, QH, HD)
        keyval = keyval.reshape(MICRO, SEQ_TOK, KVH, 2 * HD)
        queries = rotate(queries, cosine, sine_tab).astype(jnp.bfloat16)
        key_rows = rotate(keyval[..., :HD], cosine, sine_tab).astype(jnp.bfloat16)
        value_rows = keyval[..., HD:].astype(jnp.bfloat16)
        key_heads = key_rows[:, :, head_group, :].astype(jnp.float32)
        value_heads = value_rows[:, :, head_group, :].astype(jnp.float32)
        scores = jnp.einsum('mqhd,mkhd->mhqk', queries.astype(jnp.float32), key_heads) / math.sqrt(HD)
        scores = jnp.where(causal[None, None], scores, -1e+30)
        row_max = lax.optimization_barrier(jnp.max(scores, axis=-1, keepdims=True))
        expo = jnp.exp(scores - row_max)
        weights_bf = (expo / lax.optimization_barrier(jnp.sum(expo, axis=-1, keepdims=True))).astype(jnp.bfloat16)
        context = jnp.einsum('mhqk,mkhd->mqhd', weights_bf.astype(jnp.float32), value_heads).astype(jnp.bfloat16)
        update = jnp.dot(context.reshape(MICRO * SEQ_TOK, QH * HD), out_weight[layer], preferred_element_type=jnp.float32)
        hidden = (residual + update).astype(jnp.bfloat16).reshape(MICRO, SEQ_TOK, D)
        collected.append(hidden.reshape(MICRO * SEQ_TOK, D))
    return jnp.stack(collected, axis=0)
```

```python
import math

import jax
import jax.numpy as jnp
from jax import lax
from jax.experimental import pallas as pl
from jax.experimental.pallas import tpu as pltpu
from jax.sharding import Mesh
from jax.sharding import PartitionSpec as P

MICRO = 2
CORES = 2
EPS = 1e-06
THETA = 1000000.0
VMEM_LIMIT = 16 * 1024 * 1024


def to_everyone(value, axes):
    size = lax.axis_size(axes)
    return exchange(jnp.broadcast_to(value[None], (size, *value.shape)), axes)


def exchange(blocks, axes):
    return lax.all_to_all(blocks, axes, 0, 0, tiled=True)


def swap_cores(value):
    return lax.ppermute(value, "core", [(0, 1), (1, 0)])


def tables(tok_count, head_size):
    half_size = head_size // 2
    positions = jnp.arange(tok_count, dtype=jnp.float32)
    frequency = THETA ** (-jnp.arange(half_size, dtype=jnp.float32) * 2.0 / head_size)
    angles = positions[:, None] * frequency[None, :]
    cosine = jnp.concatenate([jnp.cos(angles), jnp.cos(angles)], axis=-1)
    sine = jnp.concatenate([-jnp.sin(angles), jnp.sin(angles)], axis=-1)
    return cosine, sine


def vmem_call(kernel, out_shape, name, *args):
    return pl.pallas_call(
        kernel,
        out_shape=out_shape,
        in_specs=[pl.BlockSpec(memory_space=pltpu.VMEM)] * len(args),
        out_specs=pl.BlockSpec(memory_space=pltpu.VMEM),
        compiler_params=pltpu.CompilerParams(vmem_limit_bytes=VMEM_LIMIT),
        name=name,
    )(*args)


def project_kernel(rows_ref, gain_ref, weight_ref, out_ref):
    blocks, toks, width = rows_ref.shape
    cols = weight_ref.shape[2]
    total = jnp.zeros((toks, cols), jnp.float32)
    squares = jnp.zeros((toks, width), jnp.float32)
    for i in range(blocks):
        rows = rows_ref[i].astype(jnp.float32)
        squares += rows * rows
        scaled = (rows * gain_ref[i : i + 1, :]).astype(jnp.bfloat16)
        total += jnp.dot(scaled, weight_ref[i], preferred_element_type=jnp.float32)
    out_ref[:, :cols] = total
    square_sum = jnp.sum(squares, axis=1, keepdims=True)
    out_ref[:, cols:] = jnp.broadcast_to(square_sum, (toks, out_ref.shape[1] - cols))


def attend_kernel(features, head_size, mine_ref, other_ref, bias_ref, cos_ref, sin_ref, out_ref):
    toks = mine_ref.shape[0]
    cols = bias_ref.shape[1]
    square_sum = mine_ref[:, cols:] + other_ref[:, cols:]
    inv_rms = lax.rsqrt(square_sum / features + EPS)
    cosine, sine = cos_ref[...], sin_ref[...]

    def piece(i):
        at = slice(i * head_size, (i + 1) * head_size)
        return (mine_ref[:, at] + other_ref[:, at]) * inv_rms + bias_ref[:, at]

    def rotate(values):
        turned = pltpu.roll(values, head_size // 2, 1)
        return (values * cosine + turned * sine).astype(jnp.bfloat16)

    queries = jnp.concatenate([rotate(piece(0)), rotate(piece(1))], axis=0)
    keys = rotate(piece(2))
    values = piece(3).astype(jnp.bfloat16)
    scores = lax.dot_general(
        queries, keys, (((1,), (1,)), ((), ())), preferred_element_type=jnp.float32
    )
    row = lax.broadcasted_iota(jnp.int32, scores.shape, 0) % toks
    col = lax.broadcasted_iota(jnp.int32, scores.shape, 1)
    scores = jnp.where(row >= col, scores / math.sqrt(head_size), -1e30)
    expo = jnp.exp(scores - jnp.max(scores, axis=1, keepdims=True))
    probs = (expo / jnp.sum(expo, axis=1, keepdims=True)).astype(jnp.bfloat16)
    context = jnp.dot(probs, values, preferred_element_type=jnp.float32).astype(jnp.bfloat16)
    context = jnp.concatenate([context[:toks], context[toks:]], axis=1)
    for i in range(out_ref.shape[0]):
        out_ref[i] = context


def output_kernel(context_ref, weight_ref, residual_ref, out_ref):
    total = residual_ref[...].astype(jnp.float32)
    update = jnp.zeros_like(total)
    for i in range(context_ref.shape[0]):
        update += jnp.dot(context_ref[i], weight_ref[i], preferred_element_type=jnp.float32)
    out_ref[...] = (total + update).astype(jnp.bfloat16)


def per_device(
    text_rows, image_rows, image_target, norm_gain, q_weight, q_bias, kv_weight, kv_bias, out_weight
):
    plane, chips = ("y", "core", "tp"), ("y", "tp")
    members, chip_count = lax.axis_size(plane), lax.axis_size(chips)
    ys, tps = lax.axis_size("y"), lax.axis_size("tp")
    sections = lax.axis_size("section")
    section = lax.axis_index("section")
    core = lax.axis_index("core")
    width = text_rows.shape[1]
    features = width * members
    head = q_weight.shape[2]
    toks = text_rows.shape[0] // MICRO
    own_slots = image_rows.shape[0]
    slots = own_slots * members // MICRO

    pieces = image_rows.reshape(own_slots, members, width).transpose(1, 0, 2)
    target_row = jnp.pad(image_target.astype(jnp.bfloat16), (0, width - own_slots))
    extra = jnp.zeros((8 - own_slots, width), jnp.bfloat16)
    extra = extra.at[0].set(target_row).at[1].set(norm_gain[0])
    sent = jnp.concatenate(
        [pieces, jnp.broadcast_to(extra[None], (members, *extra.shape))], axis=1
    )
    got = exchange(sent, plane)
    pictures = got[:, :own_slots].reshape(MICRO, slots, width)
    slot_grid = got[:, own_slots, :own_slots].astype(jnp.int32).reshape(MICRO, slots)
    gains = got[:, own_slots + 1].reshape(ys, CORES, tps, width)
    gain = lax.dynamic_index_in_dim(gains, core, 1, keepdims=False)
    gain = gain.reshape(chip_count, width).astype(jnp.float32)

    positions = jnp.arange(toks, dtype=jnp.int32)
    matched = slot_grid[:, None, :] == positions[None, :, None]
    placed = jnp.einsum(
        "mps,msd->mpd", matched.astype(jnp.bfloat16), pictures, preferred_element_type=jnp.float32
    )
    is_image = jnp.any(matched, axis=-1)
    text_grid = text_rows.reshape(MICRO, toks, width).astype(jnp.float32)
    embedded = jnp.where(is_image[..., None], placed, text_grid).astype(jnp.bfloat16)

    def half(weight, which):
        blocks = weight.reshape(ys, CORES, tps * width, -1)
        return lax.dynamic_index_in_dim(blocks, which, 1, keepdims=False)

    q_own = half(q_weight[0], core)
    q_other = swap_cores(half(q_weight[0], 1 - core))
    q_first = jnp.where(core == 0, q_own, q_other)
    q_second = jnp.where(core == 0, q_other, q_own)
    joint = jnp.concatenate([q_first, q_second, half(kv_weight[0], core)], axis=2)
    joint = joint.reshape(chip_count, width, 4 * head)
    own_bias = q_bias[0].astype(jnp.float32)
    other_bias = swap_cores(own_bias[None])[0]
    bias = jnp.concatenate(
        [
            jnp.where(core == 0, own_bias, other_bias),
            jnp.where(core == 0, other_bias, own_bias),
            kv_bias[0, 0].astype(jnp.float32),
        ]
    )[None]
    onward = out_weight[0].reshape(ys, CORES, tps, head, width).transpose(0, 2, 1, 3, 4)
    onward = onward.reshape(chip_count, CORES * head, width)
    cosine, sine = tables(toks, head)

    def apply_layer(current):
        gathered = to_everyone(current, chips)
        mine = vmem_call(
            project_kernel,
            jax.ShapeDtypeStruct((toks, 5 * head), jnp.float32),
            "project",
            gathered, gain, joint,
        )
        spread = vmem_call(
            lambda *refs: attend_kernel(features, head, *refs),
            jax.ShapeDtypeStruct((chip_count, toks, CORES * head), jnp.bfloat16),
            "attend",
            mine, swap_cores(mine), bias, cosine, sine,
        )
        return vmem_call(
            output_kernel,
            jax.ShapeDtypeStruct((toks, width), jnp.bfloat16),
            "output",
            exchange(spread, chips), onward, current,
        )

    ring = [(i, (i + 1) % sections) for i in range(sections)]
    stored = [jnp.zeros((toks, width), jnp.bfloat16)] * MICRO
    result = None
    for step in range(sections + MICRO - 1):
        if step == 0:
            current = embedded[0]
        else:
            current = lax.ppermute(result, "section", ring)
            if step < MICRO:
                current = jnp.where(section == 0, embedded[step], current)
        result = apply_layer(current)
        for m in range(MICRO):
            if 0 <= step - m < sections:
                stored[m] = jnp.where(section == step - m, result, stored[m])
    return jnp.concatenate(stored, axis=0)[None]


def solution(mesh):
    sections, seqs, tps = (mesh.shape[name] for name in ("section", "seq", "tp"))
    fine = Mesh(
        mesh.devices.reshape(sections, seqs // CORES, CORES, tps), ("section", "y", "core", "tp")
    )
    seq = ("y", "core")
    in_specs = (
        P(None, (*seq, "tp")),
        P((*seq, "tp"), None),
        P((*seq, "tp")),
        P("section", (*seq, "tp")),
        P("section", None, (*seq, "tp")),
        P("section", (*seq, "tp")),
        P("section", None, "tp", None),
        P("section", "tp", None),
        P("section", None, (*seq, "tp")),
    )
    out_specs = P("section", None, (*seq, "tp"))
    return jax.shard_map(
        per_device, mesh=fine, in_specs=in_specs, out_specs=out_specs, check_vma=False
    )
```

```python
import math

import jax
import jax.numpy as jnp
from jax import lax
from jax.experimental import pallas as pl
from jax.experimental.pallas import tpu as pltpu
from jax.sharding import Mesh
from jax.sharding import PartitionSpec as P

MICRO = 2
CORES = 2
EPS = 1e-06
THETA = 1000000.0
VMEM_LIMIT = 8 * 1024 * 1024


def exchange(blocks, axes):
    return lax.all_to_all(blocks, axes, 0, 0, tiled=True)


def swap_cores(value):
    return lax.ppermute(value, "core", [(0, 1), (1, 0)])


def tables(tok_count, head_size):
    half_size = head_size // 2
    positions = jnp.arange(tok_count, dtype=jnp.float32)
    frequency = THETA ** (-jnp.arange(half_size, dtype=jnp.float32) * 2.0 / head_size)
    angles = positions[:, None] * frequency[None, :]
    cosine = jnp.concatenate([jnp.cos(angles), jnp.cos(angles)], axis=-1)
    sine = jnp.concatenate([-jnp.sin(angles), jnp.sin(angles)], axis=-1)
    return cosine, sine


def vmem_call(kernel, out_shape, name, *args):
    vmem = pl.BlockSpec(memory_space=pltpu.VMEM)
    smem = pl.BlockSpec(memory_space=pltpu.SMEM)
    return pl.pallas_call(
        kernel,
        out_shape=out_shape,
        in_specs=[smem if a.dtype == jnp.int32 else vmem for a in args],
        out_specs=vmem,
        compiler_params=pltpu.CompilerParams(vmem_limit_bytes=VMEM_LIMIT),
        name=name,
    )(*args)


def attend_kernel(
    tps, head_size, rows_ref, gain_ref, query_w, keyval_w, bias_ref, cos_ref, sin_ref, out_ref
):
    chips, toks, chip_width = rows_ref.shape
    width = chip_width // CORES
    features = query_w.shape[0]
    projected = [jnp.zeros((toks, w.shape[1]), jnp.float32) for w in (query_w, keyval_w)]
    squares = jnp.zeros((toks, width), jnp.float32)
    for chip in range(chips):
        for core in range(CORES):
            block = (chip // tps * CORES + core) * tps + chip % tps
            rows = rows_ref[chip, :, core * width : (core + 1) * width].astype(jnp.float32)
            squares += rows * rows
            scaled = (rows * gain_ref[block : block + 1, :]).astype(jnp.bfloat16)
            at = slice(block * width, (block + 1) * width)
            for n, weight in enumerate((query_w, keyval_w)):
                projected[n] += jnp.dot(scaled, weight[at, :], preferred_element_type=jnp.float32)
    inv_rms = lax.rsqrt(jnp.sum(squares, axis=1, keepdims=True) / features + EPS)
    cosine, sine = cos_ref[...], sin_ref[...]

    def piece(i):
        low = i % 2 * head_size
        part = projected[i // 2][:, low : low + head_size]
        return part * inv_rms + bias_ref[:, i * head_size : (i + 1) * head_size]

    def rotate(values):
        turned = pltpu.roll(values, head_size // 2, 1)
        return (values * cosine + turned * sine).astype(jnp.bfloat16)

    queries = jnp.concatenate([rotate(piece(0)), rotate(piece(1))], axis=0)
    keys = rotate(piece(2))
    values = piece(3).astype(jnp.bfloat16)
    scores = lax.dot_general(
        queries, keys, (((1,), (1,)), ((), ())), preferred_element_type=jnp.float32
    )
    row = lax.broadcasted_iota(jnp.int32, scores.shape, 0) % toks
    col = lax.broadcasted_iota(jnp.int32, scores.shape, 1)
    scores = jnp.where(row >= col, scores / math.sqrt(head_size), -1e30)
    expo = jnp.exp(scores - jnp.max(scores, axis=1, keepdims=True))
    probs = (expo / jnp.sum(expo, axis=1, keepdims=True)).astype(jnp.bfloat16)
    context = jnp.dot(probs, values, preferred_element_type=jnp.float32).astype(jnp.bfloat16)
    context = jnp.concatenate([context[:toks], context[toks:]], axis=1)
    for i in range(chips):
        out_ref[i] = context


def output_kernel(tps, core_ref, context_ref, own_w, other_w, residual_ref, out_ref):
    chips, toks, chip_head = context_ref.shape
    head = chip_head // CORES
    width = own_w.shape[1]
    pair = 2 if tps % 2 == 0 else 1
    updates = [jnp.zeros((toks, width), jnp.float32) for _ in range(CORES)]
    for y in range(chips // tps):
        for core in range(CORES):
            for x in range(0, tps, pair):
                context = jnp.concatenate(
                    [
                        context_ref[y * tps + x + k, :, core * head : (core + 1) * head]
                        for k in range(pair)
                    ],
                    axis=1,
                )
                block = (y * CORES + core) * tps + x
                at = slice(block * head, (block + pair) * head)
                for n, weight in enumerate((own_w, other_w)):
                    updates[n] += jnp.dot(
                        context, weight[at, :], preferred_element_type=jnp.float32
                    )
    first = core_ref[0] == 0
    for n in range(CORES):
        at = slice(n * width, (n + 1) * width)
        update = jnp.where(first, updates[n], updates[1 - n])
        out_ref[:, at] = (residual_ref[:, at].astype(jnp.float32) + update).astype(jnp.bfloat16)


def per_device(
    text_rows, image_rows, image_target, norm_gain, q_weight, q_bias, kv_weight, kv_bias, out_weight
):
    plane, chips = ("y", "core", "tp"), ("y", "tp")
    members, chip_count = lax.axis_size(plane), lax.axis_size(chips)
    ys, tps = lax.axis_size("y"), lax.axis_size("tp")
    sections = lax.axis_size("section")
    section = lax.axis_index("section")
    core = lax.axis_index("core")
    width = text_rows.shape[1]
    chip_width = CORES * width
    head = q_weight.shape[2]
    toks = text_rows.shape[0] // MICRO
    own_slots = image_rows.shape[0]
    slots = own_slots * members // MICRO
    first = core == 0

    def in_order(own, other, axis):
        return jnp.concatenate(
            [jnp.where(first, own, other), jnp.where(first, other, own)], axis=axis
        )

    by_chip = image_rows.reshape(own_slots, ys, CORES, tps, width).transpose(1, 3, 0, 2, 4)
    by_chip = by_chip.reshape(ys, 1, tps, own_slots, chip_width)
    by_chip = jnp.broadcast_to(by_chip, (ys, CORES, tps, own_slots, chip_width))
    extra = jnp.concatenate(
        [
            jnp.broadcast_to(image_target.astype(jnp.bfloat16)[:, None], (own_slots, width)),
            jnp.broadcast_to(norm_gain, (own_slots, width)),
        ],
        axis=1,
    )
    extra = jnp.broadcast_to(extra, (members, own_slots, chip_width))
    sent = jnp.concatenate(
        [by_chip.reshape(members, own_slots, chip_width), extra], axis=1
    )
    got = exchange(sent, plane)
    gain = got[:, own_slots, width:].astype(jnp.float32)
    sources = members // MICRO
    own_got = lax.dynamic_slice_in_dim(got, core * sources, sources, 0)
    pictures = own_got[:, :own_slots].reshape(slots, chip_width)
    targets = own_got[:, own_slots:, 0].astype(jnp.int32).reshape(slots)

    text_grid = text_rows.reshape(MICRO, toks, width)
    text_mine = lax.dynamic_index_in_dim(text_grid, core, 0, keepdims=False)
    text_sent = lax.dynamic_index_in_dim(text_grid, 1 - core, 0, keepdims=False)
    text = in_order(text_mine, swap_cores(text_sent), 1)

    positions = jnp.arange(toks, dtype=jnp.int32)
    matched = targets[None, :] == positions[:, None]
    placed = jnp.dot(
        matched.astype(jnp.bfloat16), pictures, preferred_element_type=jnp.float32
    )
    is_image = jnp.any(matched, axis=1, keepdims=True)
    embedded = jnp.where(is_image, placed, text.astype(jnp.float32)).astype(jnp.bfloat16)

    query_w = in_order(q_weight[0], swap_cores(q_weight[0]), 1)
    keyval_w = kv_weight[0, :, 0]
    own_w = out_weight[0]
    other_w = swap_cores(own_w)
    own_bias = q_bias.astype(jnp.float32)
    bias = jnp.concatenate(
        [in_order(own_bias, swap_cores(own_bias), 1), kv_bias[0].astype(jnp.float32)], axis=1
    )
    cosine, sine = tables(toks, head)
    core_index = core[None].astype(jnp.int32)

    def apply_layer(current):
        copies = jnp.broadcast_to(current[None], (chip_count, toks, chip_width))
        spread = vmem_call(
            lambda *refs: attend_kernel(tps, head, *refs),
            jax.ShapeDtypeStruct((chip_count, toks, CORES * head), jnp.bfloat16),
            "attend",
            exchange(copies, chips), gain, query_w, keyval_w, bias, cosine, sine,
        )
        return vmem_call(
            lambda *refs: output_kernel(tps, *refs),
            jax.ShapeDtypeStruct((toks, chip_width), jnp.bfloat16),
            "output",
            core_index, exchange(spread, chips), own_w, other_w, current,
        )

    current, stored = embedded, None
    for step in range(sections):
        if step > 0:
            order = [(i + step - 1) % sections for i in range(sections)]
            pairs = list(zip(order[::2], order[1::2]))
            route = pairs + [(b, a) for a, b in pairs]
            current = lax.ppermute(current, "section", route)
        current = apply_layer(current)
        stored = current if step == 0 else jnp.where(section == step, current, stored)

    mine = jnp.where(first, stored[:, :width], stored[:, width:])
    theirs = swap_cores(jnp.where(first, stored[:, width:], stored[:, :width]))
    return in_order(mine, theirs, 0)[None]


def solution(mesh):
    sections, seqs, tps = (mesh.shape[name] for name in ("section", "seq", "tp"))
    fine = Mesh(
        mesh.devices.reshape(sections, seqs // CORES, CORES, tps), ("section", "y", "core", "tp")
    )
    seq = ("y", "core")
    in_specs = (
        P(None, (*seq, "tp")),
        P((*seq, "tp"), None),
        P((*seq, "tp")),
        P("section", (*seq, "tp")),
        P("section", None, (*seq, "tp")),
        P("section", (*seq, "tp")),
        P("section", None, "tp", None),
        P("section", "tp", None),
        P("section", None, (*seq, "tp")),
    )
    out_specs = P("section", None, (*seq, "tp"))
    return jax.shard_map(
        per_device, mesh=fine, in_specs=in_specs, out_specs=out_specs, check_vma=False
    )
```

```python
import math

import jax
import jax.numpy as jnp
from jax import lax
from jax.experimental import pallas as pl
from jax.experimental.pallas import tpu as pltpu
from jax.sharding import Mesh
from jax.sharding import PartitionSpec as P

MICRO = 2
CORES = 2
EPS = 1e-06
THETA = 1000000.0
VMEM_LIMIT = 8 * 1024 * 1024
LOAD_CHUNKS = 4
FIRST_DELAY_NS = 5000
STEP_DELAY_NS = 3700


def exchange(blocks, axes):
    return lax.all_to_all(blocks, axes, 0, 0, tiled=True)


def swap_cores(value):
    return lax.ppermute(value, "core", [(0, 1), (1, 0)])


def tables(tok_count, head_size):
    half_size = head_size // 2
    positions = jnp.arange(tok_count, dtype=jnp.float32)
    frequency = THETA ** (-jnp.arange(half_size, dtype=jnp.float32) * 2.0 / head_size)
    angles = positions[:, None] * frequency[None, :]
    cosine = jnp.concatenate([jnp.cos(angles), jnp.cos(angles)], axis=-1)
    sine = jnp.concatenate([-jnp.sin(angles), jnp.sin(angles)], axis=-1)
    return cosine, sine


def vmem_call(kernel, out_shape, name, *args, hbm=(), scratch=()):
    vmem = pl.BlockSpec(memory_space=pltpu.VMEM)
    smem = pl.BlockSpec(memory_space=pltpu.SMEM)
    return pl.pallas_call(
        kernel,
        out_shape=out_shape,
        in_specs=[smem if a.dtype == jnp.int32 else vmem for a in args]
        + [pl.BlockSpec(memory_space=pltpu.HBM)] * len(hbm),
        out_specs=jax.tree.map(lambda _: vmem, out_shape),
        scratch_shapes=list(scratch),
        compiler_params=pltpu.CompilerParams(vmem_limit_bytes=VMEM_LIMIT),
        name=name,
    )(*args, *(pltpu.with_memory_space_constraint(a, pltpu.HBM) for a in hbm))


def pack_kernel(
    ys, tps, target_ref, image_hbm, gain_hbm, bias_hbm, out_ref, image_ref, gain_ref, bias_ref, sems
):
    copies = [
        pltpu.make_async_copy(src, dst, sems.at[i])
        for i, (src, dst) in enumerate(
            ((image_hbm, image_ref), (gain_hbm, gain_ref), (bias_hbm, bias_ref))
        )
    ]
    for copy in copies:
        copy.start()
    slots = image_ref.shape[0]
    width = gain_ref.shape[1]
    head = bias_ref.shape[1]
    at_row = lax.broadcasted_iota(jnp.int32, (slots, width), 0)
    targets = jnp.zeros((slots, width), jnp.int32)
    for i in range(slots):
        targets = jnp.where(at_row == i, target_ref[i], targets)
    targets = targets.astype(jnp.float32).astype(jnp.bfloat16)
    for copy in copies:
        copy.wait()
    bias = jnp.concatenate([bias_ref[...].astype(jnp.float32)] * (width // head), axis=1)
    gain = gain_ref[...].astype(jnp.float32)
    extra = jnp.where(at_row == slots - 1, gain, bias).astype(jnp.bfloat16)
    for y in range(ys):
        for x in range(tps):
            for core in range(CORES):
                member = (y * CORES + core) * tps + x
                for n in range(CORES):
                    at = slice(n * width, (n + 1) * width)
                    block = (y * CORES + n) * tps + x
                    columns = slice(block * width, (block + 1) * width)
                    out_ref[member, :slots, at] = image_ref[:, columns]
                out_ref[member, slots:, :width] = targets
                out_ref[member, slots:, width:] = extra


def embed_kernel(own_slots, place_ref, got_ref, text_ref, other_ref, rows_ref, out_ref):
    members, tile, chip_width = got_ref.shape
    toks = rows_ref.shape[0]
    width = chip_width // CORES
    core = place_ref[0]
    pl.delay((1 - core) * FIRST_DELAY_NS)
    sources = members // MICRO
    picked = got_ref[pl.ds(core * sources, sources)].reshape(sources * tile, chip_width)
    lanes = picked[:, :128].astype(jnp.float32)
    targets = pltpu.roll(lanes, sources * tile - own_slots, 0)
    row = lax.broadcasted_iota(jnp.int32, lanes.shape, 0)
    col = lax.broadcasted_iota(jnp.int32, lanes.shape, 1).astype(jnp.float32)
    matched = jnp.where(row % tile < own_slots, (targets == col).astype(jnp.float32), 0.0)
    matched = matched.astype(jnp.bfloat16)
    over_rows = (((0,), (0,)), ((), ()))
    placed = lax.dot_general(matched, picked, over_rows, preferred_element_type=jnp.float32)[:toks]
    counts = lax.dot_general(
        matched,
        jnp.ones((sources * tile, width), jnp.bfloat16),
        over_rows,
        preferred_element_type=jnp.float32,
    )[:toks]
    at = pl.ds(pl.multiple_of(core * toks, toks), toks)
    mine, theirs = text_ref[at, :].astype(jnp.float32), other_ref[at, :].astype(jnp.float32)
    first = core == 0
    for n in range(CORES):
        text = jnp.where(first, mine, theirs) if n == 0 else jnp.where(first, theirs, mine)
        half = slice(n * width, (n + 1) * width)
        rows_ref[:, half] = jnp.where(counts > 0.5, placed[:, half], text).astype(jnp.bfloat16)
    rows = rows_ref[...]
    for i in range(out_ref.shape[0]):
        out_ref[i] = rows


def attend_kernel(
    tps, head_size, place_ref, rows_ref, got_ref, query_w, keyval_w, bias_ref, cos_ref, sin_ref,
    *refs, before=None
):
    out_ref = refs[0]
    chips, toks, chip_width = rows_ref.shape
    width = chip_width // CORES
    features = query_w.shape[0]
    projected = [jnp.zeros((toks, w.shape[1]), jnp.float32) for w in (query_w, keyval_w)]
    squares = jnp.zeros((toks, width), jnp.float32)
    for block in range(chips * CORES):
        if before is not None:
            before(block)
        y, core, x = block // (CORES * tps), block // tps % CORES, block % tps
        gain = got_ref[block, :, width:].astype(jnp.float32)[-1:]
        rows = rows_ref[y * tps + x, :, core * width : (core + 1) * width].astype(jnp.float32)
        squares += rows * rows
        scaled = (rows * gain).astype(jnp.bfloat16)
        at = slice(block * width, (block + 1) * width)
        for n, weight in enumerate((query_w, keyval_w)):
            projected[n] += jnp.dot(scaled, weight[at, :], preferred_element_type=jnp.float32)
    inv_rms = lax.rsqrt(jnp.sum(squares, axis=1, keepdims=True) / features + EPS)
    cosine, sine = cos_ref[...], sin_ref[...]
    tile = got_ref.shape[1]
    biases = [
        got_ref[place_ref[2] + i * tps, :, width : width + head_size].astype(jnp.float32)[
            tile // 2 : tile // 2 + 1
        ]
        for i in range(CORES)
    ]
    biases += [
        bias_ref[:, i * head_size : (i + 1) * head_size].astype(jnp.float32) for i in range(2)
    ]

    def piece(i):
        low = i % 2 * head_size
        return projected[i // 2][:, low : low + head_size] * inv_rms + biases[i]

    def rotate(values):
        turned = pltpu.roll(values, head_size // 2, 1)
        return (values * cosine + turned * sine).astype(jnp.bfloat16)

    queries = jnp.concatenate([rotate(piece(0)), rotate(piece(1))], axis=0)
    keys = rotate(piece(2))
    values = piece(3).astype(jnp.bfloat16)
    scores = lax.dot_general(
        queries, keys, (((1,), (1,)), ((), ())), preferred_element_type=jnp.float32
    )
    row = lax.broadcasted_iota(jnp.int32, scores.shape, 0) % toks
    col = lax.broadcasted_iota(jnp.int32, scores.shape, 1)
    scores = jnp.where(row >= col, scores / math.sqrt(head_size), -1e30)
    expo = jnp.exp(scores - jnp.max(scores, axis=1, keepdims=True))
    probs = (expo / jnp.sum(expo, axis=1, keepdims=True)).astype(jnp.bfloat16)
    context = jnp.dot(probs, values, preferred_element_type=jnp.float32).astype(jnp.bfloat16)
    context = jnp.concatenate([context[:toks], context[toks:]], axis=1)
    for i in range(chips):
        out_ref[i] = context


def first_attend_kernel(
    tps, head_size, place_ref, rows_ref, got_ref, bias_ref, cos_ref, sin_ref,
    own_q, other_q, keyval_hbm, out_ref, query_w, keyval_w, sems
):
    features = query_w.shape[0]
    part = features // LOAD_CHUNKS
    core = place_ref[0]
    copies = []
    for i in range(LOAD_CHUNKS):
        at = pl.ds(i * part, part)
        own = pl.ds(pl.multiple_of(core * head_size, head_size), head_size)
        other = pl.ds(pl.multiple_of((1 - core) * head_size, head_size), head_size)
        copies.append(
            [
                pltpu.make_async_copy(own_q.at[at], query_w.at[at, own], sems.at[i, 0]),
                pltpu.make_async_copy(other_q.at[at], query_w.at[at, other], sems.at[i, 1]),
                pltpu.make_async_copy(keyval_hbm.at[at], keyval_w.at[at], sems.at[i, 2]),
            ]
        )
    for group in copies:
        for copy in group:
            copy.start()
    blocks = rows_ref.shape[0] * CORES

    def before(block):
        if block % (blocks // LOAD_CHUNKS) == 0:
            for copy in copies[block // (blocks // LOAD_CHUNKS)]:
                copy.wait()

    attend_kernel(
        tps, head_size, place_ref, rows_ref, got_ref, query_w, keyval_w, bias_ref, cos_ref, sin_ref,
        out_ref, before=before,
    )


def output_kernel(tps, step, last, place_ref, context_ref, own_w, other_w, residual_ref, *refs):
    out_ref, keep_ref = refs[-2:]
    pl.delay(place_ref[0] * STEP_DELAY_NS)
    chips, toks, chip_head = context_ref.shape
    head = chip_head // CORES
    width = own_w.shape[1]
    pair = 2 if tps % 2 == 0 else 1
    updates = [jnp.zeros((toks, width), jnp.float32) for _ in range(CORES)]
    for y in range(chips // tps):
        for core in range(CORES):
            for x in range(0, tps, pair):
                context = jnp.concatenate(
                    [
                        context_ref[y * tps + x + k, :, core * head : (core + 1) * head]
                        for k in range(pair)
                    ],
                    axis=1,
                )
                block = (y * CORES + core) * tps + x
                at = slice(block * head, (block + pair) * head)
                for n, weight in enumerate((own_w, other_w)):
                    updates[n] += jnp.dot(
                        context, weight[at, :], preferred_element_type=jnp.float32
                    )
    first = place_ref[0] == 0
    kept = []
    for n in range(CORES):
        at = slice(n * width, (n + 1) * width)
        update = jnp.where(first, updates[n], updates[1 - n])
        result = (residual_ref[:, at].astype(jnp.float32) + update).astype(jnp.bfloat16)
        kept.append(result if step == 0 else jnp.where(place_ref[1] == step, result, refs[0][:, at]))
        if last:
            continue
        out_ref[:, at] = result
        keep_ref[:, at] = kept[n]
    if last:
        out_ref[...] = jnp.where(first, kept[0], kept[1])
        keep_ref[...] = jnp.where(first, kept[1], kept[0])


def join_kernel(place_ref, mine_ref, theirs_ref, out_ref):
    toks = mine_ref.shape[0]
    core = place_ref[0]
    out_ref[pl.ds(pl.multiple_of(core * toks, toks), toks), :] = mine_ref[...]
    out_ref[pl.ds(pl.multiple_of((1 - core) * toks, toks), toks), :] = theirs_ref[...]


def per_device(
    text_rows, image_rows, image_target, norm_gain, q_weight, q_bias, kv_weight, kv_bias, out_weight
):
    plane, chips = ("y", "core", "tp"), ("y", "tp")
    members, chip_count = lax.axis_size(plane), lax.axis_size(chips)
    ys, tps = lax.axis_size("y"), lax.axis_size("tp")
    sections = lax.axis_size("section")
    section = lax.axis_index("section")
    core = lax.axis_index("core")
    width = text_rows.shape[1]
    chip_width = CORES * width
    head = q_weight.shape[2]
    features = q_weight.shape[1]
    toks = text_rows.shape[0] // MICRO
    own_slots = image_rows.shape[0]
    sent = vmem_call(
        lambda *refs: pack_kernel(ys, tps, *refs),
        jax.ShapeDtypeStruct((members, 2 * own_slots, chip_width), jnp.bfloat16),
        "pack",
        image_target,
        hbm=(image_rows, norm_gain, q_bias),
        scratch=[
            pltpu.VMEM(a.shape, a.dtype) for a in (image_rows, norm_gain, q_bias)
        ]
        + [pltpu.SemaphoreType.DMA((3,))],
    )
    got = exchange(sent, plane)
    other_text = swap_cores(text_rows)
    other_q = swap_cores(q_weight[0])
    own_w = out_weight[0]
    other_w = swap_cores(own_w)
    cosine, sine = tables(toks, head)
    chip = lax.axis_index("y") * CORES * tps + lax.axis_index("tp")
    place = jnp.stack([core, section, chip]).astype(jnp.int32)
    got, other_text, other_q, other_w, cosine, sine, place = lax.optimization_barrier(
        (got, other_text, other_q, other_w, cosine, sine, place)
    )

    rows = jax.ShapeDtypeStruct((toks, chip_width), jnp.bfloat16)
    text_half = jax.ShapeDtypeStruct((toks, width), jnp.bfloat16)
    copies = jax.ShapeDtypeStruct((chip_count, toks, chip_width), jnp.bfloat16)
    contexts = jax.ShapeDtypeStruct((chip_count, toks, CORES * head), jnp.bfloat16)
    weights = jax.ShapeDtypeStruct((features, CORES * head), jnp.bfloat16)
    current, sent = vmem_call(
        lambda *refs: embed_kernel(own_slots, *refs),
        (rows, copies),
        "embed",
        place, got, text_rows, other_text,
    )
    stored = ()
    for step in range(sections):
        if step > 0:
            route = [(i, i) for i in range(sections)]
            route[step - 1], route[step] = (step - 1, step), (step, step - 1)
            current = lax.ppermute(current, "section", route)
            sent = jnp.broadcast_to(current[None], copies.shape)
        gathered = exchange(sent, chips)
        if step == 0:
            context, query_w, keyval_w = vmem_call(
                lambda *refs: first_attend_kernel(tps, head, *refs),
                (contexts, weights, weights),
                "attend_first",
                place, gathered, got, kv_bias[0], cosine, sine,
                hbm=(q_weight[0], other_q, kv_weight[0, :, 0]),
                scratch=[pltpu.SemaphoreType.DMA((LOAD_CHUNKS, 3))],
            )
        else:
            context = vmem_call(
                lambda *refs: attend_kernel(tps, head, *refs),
                contexts,
                "attend",
                place, gathered, got, query_w, keyval_w, kv_bias[0], cosine, sine,
            )
        last = step == sections - 1
        out = text_half if last else rows
        current, keep = vmem_call(
            lambda *refs: output_kernel(tps, step, last, *refs),
            (out, out),
            "output",
            place, exchange(context, chips), own_w, other_w, current, *stored,
        )
        stored = (keep,)
    joined = jax.ShapeDtypeStruct((MICRO * toks, width), jnp.bfloat16)
    return vmem_call(join_kernel, joined, "join", place, current, swap_cores(keep))[None]


def solution(mesh):
    sections, seqs, tps = (mesh.shape[name] for name in ("section", "seq", "tp"))
    fine = Mesh(
        mesh.devices.reshape(sections, seqs // CORES, CORES, tps), ("section", "y", "core", "tp")
    )
    seq = ("y", "core")
    in_specs = (
        P(None, (*seq, "tp")),
        P((*seq, "tp"), None),
        P((*seq, "tp")),
        P("section", (*seq, "tp")),
        P("section", None, (*seq, "tp")),
        P("section", (*seq, "tp")),
        P("section", None, "tp", None),
        P("section", "tp", None),
        P("section", None, (*seq, "tp")),
    )
    out_specs = P("section", None, (*seq, "tp"))
    return jax.shard_map(
        per_device, mesh=fine, in_specs=in_specs, out_specs=out_specs, check_vma=False
    )
```

```python
import math

import jax
import jax.numpy as jnp
from jax import lax
from jax.experimental import pallas as pl
from jax.experimental.pallas import tpu as pltpu
from jax.sharding import Mesh
from jax.sharding import PartitionSpec as P

MICRO = 2
CORES = 2
EPS = 1e-06
THETA = 1000000.0
VMEM_LIMIT = 8 * 1024 * 1024
LOAD_CHUNKS = 4
FIRST_DELAY_NS = 5000
STEP_DELAY_NS = 3500


def exchange(blocks, axes):
    return lax.all_to_all(blocks, axes, 0, 0, tiled=True)


def swap_cores(value):
    return lax.ppermute(value, "core", [(0, 1), (1, 0)])


def tables(tok_count, head_size):
    half_size = head_size // 2
    positions = jnp.arange(tok_count, dtype=jnp.float32)
    frequency = THETA ** (-jnp.arange(half_size, dtype=jnp.float32) * 2.0 / head_size)
    angles = positions[:, None] * frequency[None, :]
    cosine = jnp.concatenate([jnp.cos(angles), jnp.cos(angles)], axis=-1)
    sine = jnp.concatenate([-jnp.sin(angles), jnp.sin(angles)], axis=-1)
    return cosine, sine


def vmem_call(kernel, out_shape, name, *args, hbm=(), scratch=()):
    vmem = pl.BlockSpec(memory_space=pltpu.VMEM)
    smem = pl.BlockSpec(memory_space=pltpu.SMEM)
    return pl.pallas_call(
        kernel,
        out_shape=out_shape,
        in_specs=[smem if a.dtype == jnp.int32 else vmem for a in args]
        + [pl.BlockSpec(memory_space=pltpu.HBM)] * len(hbm),
        out_specs=jax.tree.map(lambda _: vmem, out_shape),
        scratch_shapes=list(scratch),
        compiler_params=pltpu.CompilerParams(vmem_limit_bytes=VMEM_LIMIT),
        name=name,
    )(*args, *(pltpu.with_memory_space_constraint(a, pltpu.HBM) for a in hbm))


def pack_kernel(
    ys, tps, target_hbm, image_hbm, gain_hbm, bias_hbm,
    out_ref, target_ref, image_ref, gain_ref, bias_ref, sems,
):
    copies = [
        pltpu.make_async_copy(src, dst, sems.at[i])
        for i, (src, dst) in enumerate(
            (
                (target_hbm, target_ref),
                (image_hbm, image_ref),
                (gain_hbm, gain_ref),
                (bias_hbm, bias_ref),
            )
        )
    ]
    for copy in copies:
        copy.start()
    slots = image_ref.shape[0]
    width = gain_ref.shape[1]
    head = bias_ref.shape[1]
    at_row = lax.broadcasted_iota(jnp.int32, (slots, width), 0)
    for copy in copies:
        copy.wait()
    targets = jnp.zeros((slots, width), jnp.int32)
    for i in range(slots):
        targets = jnp.where(at_row == i, target_ref[i], targets)
    targets = targets.astype(jnp.float32).astype(jnp.bfloat16)
    bias = jnp.concatenate([bias_ref[...].astype(jnp.float32)] * (width // head), axis=1)
    gain = gain_ref[...].astype(jnp.float32)
    extra = jnp.where(at_row == slots - 1, gain, bias).astype(jnp.bfloat16)
    for y in range(ys):
        for x in range(tps):
            for core in range(CORES):
                member = (y * CORES + core) * tps + x
                for n in range(CORES):
                    at = slice(n * width, (n + 1) * width)
                    block = (y * CORES + n) * tps + x
                    columns = slice(block * width, (block + 1) * width)
                    out_ref[member, :slots, at] = image_ref[:, columns]
                out_ref[member, slots:, :width] = targets
                out_ref[member, slots:, width:] = extra


def embed_kernel(
    own_slots, place_ref, got_ref, other_ref, text_hbm, rows_ref, out_ref, text_ref, sem
):
    text_copy = pltpu.make_async_copy(text_hbm, text_ref, sem)
    text_copy.start()
    members, tile, chip_width = got_ref.shape
    toks = rows_ref.shape[0]
    width = chip_width // CORES
    core = place_ref[0]
    pl.delay((1 - core) * FIRST_DELAY_NS)
    sources = members // MICRO
    picked = got_ref[pl.ds(core * sources, sources)].reshape(sources * tile, chip_width)
    lanes = picked[:, :128].astype(jnp.float32)
    targets = pltpu.roll(lanes, sources * tile - own_slots, 0)
    row = lax.broadcasted_iota(jnp.int32, lanes.shape, 0)
    col = lax.broadcasted_iota(jnp.int32, lanes.shape, 1).astype(jnp.float32)
    matched = jnp.where(row % tile < own_slots, (targets == col).astype(jnp.float32), 0.0)
    matched = matched.astype(jnp.bfloat16)
    over_rows = (((0,), (0,)), ((), ()))
    placed = lax.dot_general(matched, picked, over_rows, preferred_element_type=jnp.float32)[:toks]
    counts = lax.dot_general(
        matched,
        jnp.ones((sources * tile, width), jnp.bfloat16),
        over_rows,
        preferred_element_type=jnp.float32,
    )[:toks]
    at = pl.ds(pl.multiple_of(core * toks, toks), toks)
    text_copy.wait()
    mine, theirs = text_ref[at, :].astype(jnp.float32), other_ref[at, :].astype(jnp.float32)
    first = core == 0
    for n in range(CORES):
        text = jnp.where(first, mine, theirs) if n == 0 else jnp.where(first, theirs, mine)
        half = slice(n * width, (n + 1) * width)
        rows_ref[:, half] = jnp.where(counts > 0.5, placed[:, half], text).astype(jnp.bfloat16)
    rows = rows_ref[...]
    for i in range(out_ref.shape[0]):
        out_ref[i] = rows


def attend_kernel(tps, head_size, step, place_ref, *refs):
    @pl.when(place_ref[1] == step)
    def _():
        attend(tps, head_size, *refs)


def attend(
    tps, head_size, rows_ref, gain_ref, query_w, keyval_w, bias_ref, cos_ref, sin_ref, out_ref,
    before=None
):
    chips, toks, chip_width = rows_ref.shape
    width = chip_width // CORES
    features = query_w.shape[0]
    projected = [jnp.zeros((toks, w.shape[1]), jnp.float32) for w in (query_w, keyval_w)]
    squares = jnp.zeros((toks, width), jnp.float32)
    for block in range(chips * CORES):
        if before is not None:
            before(block)
        y, core, x = block // (CORES * tps), block // tps % CORES, block % tps
        gain = gain_ref[block : block + 1, :]
        rows = rows_ref[y * tps + x, :, core * width : (core + 1) * width].astype(jnp.float32)
        squares += rows * rows
        scaled = (rows * gain).astype(jnp.bfloat16)
        at = slice(block * width, (block + 1) * width)
        for n, weight in enumerate((query_w, keyval_w)):
            projected[n] += jnp.dot(scaled, weight[at, :], preferred_element_type=jnp.float32)
    inv_rms = lax.rsqrt(jnp.sum(squares, axis=1, keepdims=True) / features + EPS)
    cosine, sine = cos_ref[...], sin_ref[...]

    def piece(i):
        low = i % 2 * head_size
        return projected[i // 2][:, low : low + head_size] * inv_rms + bias_ref[
            :, i * head_size : (i + 1) * head_size
        ]

    def rotate(values):
        turned = pltpu.roll(values, head_size // 2, 1)
        return (values * cosine + turned * sine).astype(jnp.bfloat16)

    queries = jnp.concatenate([rotate(piece(0)), rotate(piece(1))], axis=0)
    keys = rotate(piece(2))
    values = piece(3).astype(jnp.bfloat16)
    scores = lax.dot_general(
        queries, keys, (((1,), (1,)), ((), ())), preferred_element_type=jnp.float32
    )
    row = lax.broadcasted_iota(jnp.int32, scores.shape, 0) % toks
    col = lax.broadcasted_iota(jnp.int32, scores.shape, 1)
    scores = jnp.where(row >= col, scores / math.sqrt(head_size), -1e30)
    expo = jnp.exp(scores - jnp.max(scores, axis=1, keepdims=True))
    probs = (expo / jnp.sum(expo, axis=1, keepdims=True)).astype(jnp.bfloat16)
    context = jnp.dot(probs, values, preferred_element_type=jnp.float32).astype(jnp.bfloat16)
    context = jnp.concatenate([context[:toks], context[toks:]], axis=1)
    for i in range(chips):
        out_ref[i] = context


def first_attend_kernel(
    tps, head_size, place_ref, rows_ref, got_ref, bias_ref, cos_ref, sin_ref,
    own_q, other_q, keyval_hbm, out_ref, query_w, keyval_w, gain_out, bias_out, sems
):
    features = query_w.shape[0]
    part = features // LOAD_CHUNKS
    core = place_ref[0]
    copies = []
    for i in range(LOAD_CHUNKS):
        at = pl.ds(i * part, part)
        own = pl.ds(pl.multiple_of(core * head_size, head_size), head_size)
        other = pl.ds(pl.multiple_of((1 - core) * head_size, head_size), head_size)
        copies.append(
            [
                pltpu.make_async_copy(own_q.at[at], query_w.at[at, own], sems.at[i, 0]),
                pltpu.make_async_copy(other_q.at[at], query_w.at[at, other], sems.at[i, 1]),
                pltpu.make_async_copy(keyval_hbm.at[at], keyval_w.at[at], sems.at[i, 2]),
            ]
        )
    for group in copies:
        for copy in group:
            copy.start()
    blocks = rows_ref.shape[0] * CORES

    def before(block):
        if block % (blocks // LOAD_CHUNKS) == 0:
            for copy in copies[block // (blocks // LOAD_CHUNKS)]:
                copy.wait()

    width = gain_out.shape[1]
    tile = got_ref.shape[1]
    for block in range(blocks):
        gain = got_ref[block, :, width:].astype(jnp.float32)
        gain_out[block : block + 1, :] = gain[tile - 1 :]
    for i in range(CORES):
        own = got_ref[place_ref[2] + i * tps, :, width : width + head_size].astype(jnp.float32)
        bias_out[:, i * head_size : (i + 1) * head_size] = own[tile // 2 : tile // 2 + 1]
    bias_out[:, CORES * head_size :] = bias_ref[...].astype(jnp.float32)
    active = place_ref[1] == 0

    @pl.when(active)
    def _():
        attend(
            tps, head_size, rows_ref, gain_out, query_w, keyval_w, bias_out, cos_ref, sin_ref,
            out_ref, before=before,
        )

    @pl.when(jnp.logical_not(active))
    def _():
        for block in range(blocks):
            before(block)


def output_kernel(
    tps, step, last, place_ref, context_ref, own_w, other_w, residual_ref, *refs
):
    out_ref, keep_ref = refs[-2:]
    chips, toks, chip_head = context_ref.shape
    head = chip_head // CORES
    width = own_w.shape[1]
    halves = [slice(n * width, (n + 1) * width) for n in range(CORES)]
    pair = 2 if tps % 2 == 0 else 1
    first = place_ref[0] == 0
    active = place_ref[1] == step

    def keep(kept):
        if last:
            out_ref[...] = jnp.where(first, kept[0], kept[1])
            keep_ref[...] = jnp.where(first, kept[1], kept[0])
        else:
            for at, half in zip(halves, kept):
                keep_ref[:, at] = half

    @pl.when(active)
    def _():
        pl.delay(place_ref[0] * STEP_DELAY_NS)
        updates = [jnp.zeros((toks, width), jnp.float32) for _ in range(CORES)]
        for y in range(chips // tps):
            for core in range(CORES):
                for x in range(0, tps, pair):
                    context = jnp.concatenate(
                        [
                            context_ref[y * tps + x + k, :, core * head : (core + 1) * head]
                            for k in range(pair)
                        ],
                        axis=1,
                    )
                    block = (y * CORES + core) * tps + x
                    at = slice(block * head, (block + pair) * head)
                    for n, weight in enumerate((own_w, other_w)):
                        updates[n] += jnp.dot(
                            context, weight[at, :], preferred_element_type=jnp.float32
                        )
        results = []
        for n, at in enumerate(halves):
            update = jnp.where(first, updates[n], updates[1 - n])
            result = (residual_ref[:, at].astype(jnp.float32) + update).astype(jnp.bfloat16)
            results.append(result)
            if not last:
                out_ref[:, at] = result
        keep(results)

    if step > 0:

        @pl.when(jnp.logical_not(active))
        def _():
            keep([refs[0][:, at] for at in halves])


def join_kernel(place_ref, mine_ref, theirs_ref, out_ref):
    toks = mine_ref.shape[0]
    core = place_ref[0]
    out_ref[pl.ds(pl.multiple_of(core * toks, toks), toks), :] = mine_ref[...]
    out_ref[pl.ds(pl.multiple_of((1 - core) * toks, toks), toks), :] = theirs_ref[...]


def per_device(
    text_rows, image_rows, image_target, norm_gain, q_weight, q_bias, kv_weight, kv_bias, out_weight
):
    plane, chips = ("y", "core", "tp"), ("y", "tp")
    members, chip_count = lax.axis_size(plane), lax.axis_size(chips)
    ys, tps = lax.axis_size("y"), lax.axis_size("tp")
    sections = lax.axis_size("section")
    section = lax.axis_index("section")
    core = lax.axis_index("core")
    width = text_rows.shape[1]
    chip_width = CORES * width
    head = q_weight.shape[2]
    features = q_weight.shape[1]
    toks = text_rows.shape[0] // MICRO
    own_slots = image_rows.shape[0]
    sent = vmem_call(
        lambda *refs: pack_kernel(ys, tps, *refs),
        jax.ShapeDtypeStruct((members, 2 * own_slots, chip_width), jnp.bfloat16),
        "pack",
        hbm=(image_target, image_rows, norm_gain, q_bias),
        scratch=[pltpu.SMEM(image_target.shape, jnp.int32)]
        + [pltpu.VMEM(a.shape, a.dtype) for a in (image_rows, norm_gain, q_bias)]
        + [pltpu.SemaphoreType.DMA((4,))],
    )
    got = exchange(sent, plane)
    other_text = swap_cores(text_rows)
    other_q = swap_cores(q_weight[0])
    own_w = out_weight[0]
    other_w = swap_cores(own_w)
    cosine, sine = tables(toks, head)
    chip = lax.axis_index("y") * CORES * tps + lax.axis_index("tp")
    place = jnp.stack([core, section, chip]).astype(jnp.int32)
    got, other_text, other_q, other_w, cosine, sine, place = lax.optimization_barrier(
        (got, other_text, other_q, other_w, cosine, sine, place)
    )

    rows = jax.ShapeDtypeStruct((toks, chip_width), jnp.bfloat16)
    text_half = jax.ShapeDtypeStruct((toks, width), jnp.bfloat16)
    copies = jax.ShapeDtypeStruct((chip_count, toks, chip_width), jnp.bfloat16)
    contexts = jax.ShapeDtypeStruct((chip_count, toks, CORES * head), jnp.bfloat16)
    weights = jax.ShapeDtypeStruct((features, CORES * head), jnp.bfloat16)
    current, sent = vmem_call(
        lambda *refs: embed_kernel(own_slots, *refs),
        (rows, copies),
        "embed",
        place, got, other_text,
        hbm=(text_rows,),
        scratch=[pltpu.VMEM(text_rows.shape, text_rows.dtype), pltpu.SemaphoreType.DMA],
    )
    stored = ()
    for step in range(sections):
        if step > 0:
            order = [(i + step - 1) % sections for i in range(sections)]
            pairs = list(zip(order[::2], order[1::2]))
            route = pairs + [(b, a) for a, b in pairs]
            current = lax.ppermute(current, "section", route)
            sent = jnp.broadcast_to(current[None], copies.shape)
        gathered = exchange(sent, chips)
        if step == 0:
            context, query_w, keyval_w, gain, bias = vmem_call(
                lambda *refs: first_attend_kernel(tps, head, *refs),
                (
                    contexts,
                    weights,
                    weights,
                    jax.ShapeDtypeStruct((members, width), jnp.float32),
                    jax.ShapeDtypeStruct((1, 2 * CORES * head), jnp.float32),
                ),
                "attend_first",
                place, gathered, got, kv_bias[0], cosine, sine,
                hbm=(q_weight[0], other_q, kv_weight[0, :, 0]),
                scratch=[pltpu.SemaphoreType.DMA((LOAD_CHUNKS, 3))],
            )
        else:
            context = vmem_call(
                lambda *refs: attend_kernel(tps, head, step, *refs),
                contexts,
                "attend",
                place, gathered, gain, query_w, keyval_w, bias, cosine, sine,
            )
        last = step == sections - 1
        out = text_half if last else rows
        current, keep = vmem_call(
            lambda *refs: output_kernel(tps, step, last, *refs),
            (out, out),
            "output",
            place, exchange(context, chips), own_w, other_w, current, *stored,
        )
        stored = (keep,)
    joined = jax.ShapeDtypeStruct((MICRO * toks, width), jnp.bfloat16)
    return vmem_call(join_kernel, joined, "join", place, current, swap_cores(keep))[None]


def solution(mesh):
    sections, seqs, tps = (mesh.shape[name] for name in ("section", "seq", "tp"))
    fine = Mesh(
        mesh.devices.reshape(sections, seqs // CORES, CORES, tps), ("section", "y", "core", "tp")
    )
    seq = ("y", "core")
    in_specs = (
        P(None, (*seq, "tp")),
        P((*seq, "tp"), None),
        P((*seq, "tp")),
        P("section", (*seq, "tp")),
        P("section", None, (*seq, "tp")),
        P("section", (*seq, "tp")),
        P("section", None, "tp", None),
        P("section", "tp", None),
        P("section", None, (*seq, "tp")),
    )
    out_specs = P("section", None, (*seq, "tp"))
    return jax.shard_map(
        per_device, mesh=fine, in_specs=in_specs, out_specs=out_specs, check_vma=False
    )
```

```python
import math

import jax
import jax.numpy as jnp
from jax import lax
from jax.experimental import pallas as pl
from jax.experimental.pallas import tpu as pltpu
from jax.sharding import Mesh
from jax.sharding import PartitionSpec as P

MICRO = 2
CORES = 2
EPS = 1e-06
THETA = 1000000.0
VMEM_LIMIT = 8 * 1024 * 1024
LOAD_CHUNKS = 4
FIRST_DELAY_NS = 5000
STEP_DELAY_NS = 3500


def exchange(blocks, axes):
    return lax.all_to_all(blocks, axes, 0, 0, tiled=True)


def swap_cores(value):
    return lax.ppermute(value, "core", [(0, 1), (1, 0)])


def tables(tok_count, head_size):
    half_size = head_size // 2
    positions = jnp.arange(tok_count, dtype=jnp.float32)
    frequency = THETA ** (-jnp.arange(half_size, dtype=jnp.float32) * 2.0 / head_size)
    angles = positions[:, None] * frequency[None, :]
    cosine = jnp.concatenate([jnp.cos(angles), jnp.cos(angles)], axis=-1)
    sine = jnp.concatenate([-jnp.sin(angles), jnp.sin(angles)], axis=-1)
    return cosine, sine


def vmem_call(kernel, out_shape, name, *args, hbm=(), scratch=()):
    vmem = pl.BlockSpec(memory_space=pltpu.VMEM)
    return pl.pallas_call(
        kernel,
        out_shape=out_shape,
        in_specs=[vmem] * len(args)
        + [pl.BlockSpec(memory_space=pltpu.HBM)] * len(hbm),
        out_specs=jax.tree.map(lambda _: vmem, out_shape),
        scratch_shapes=list(scratch),
        compiler_params=pltpu.CompilerParams(vmem_limit_bytes=VMEM_LIMIT),
        name=name,
    )(*args, *(pltpu.with_memory_space_constraint(a, pltpu.HBM) for a in hbm))


def pack_kernel(
    ys, tps, target_hbm, image_hbm, gain_hbm, bias_hbm,
    out_ref, target_ref, image_ref, gain_ref, bias_ref, sems,
):
    copies = [
        pltpu.make_async_copy(src, dst, sems.at[i])
        for i, (src, dst) in enumerate(
            (
                (target_hbm, target_ref),
                (image_hbm, image_ref),
                (gain_hbm, gain_ref),
                (bias_hbm, bias_ref),
            )
        )
    ]
    for copy in copies:
        copy.start()
    slots = image_ref.shape[0]
    width = gain_ref.shape[1]
    head = bias_ref.shape[1]
    at_row = lax.broadcasted_iota(jnp.int32, (slots, width), 0)
    for copy in copies:
        copy.wait()
    targets = jnp.zeros((slots, width), jnp.int32)
    for i in range(slots):
        targets = jnp.where(at_row == i, target_ref[i], targets)
    targets = targets.astype(jnp.float32).astype(jnp.bfloat16)
    bias = jnp.concatenate([bias_ref[...].astype(jnp.float32)] * (width // head), axis=1)
    gain = gain_ref[...].astype(jnp.float32)
    extra = jnp.where(at_row == slots - 1, gain, bias).astype(jnp.bfloat16)
    for y in range(ys):
        for x in range(tps):
            for core in range(CORES):
                member = (y * CORES + core) * tps + x
                for n in range(CORES):
                    at = slice(n * width, (n + 1) * width)
                    block = (y * CORES + n) * tps + x
                    columns = slice(block * width, (block + 1) * width)
                    out_ref[member, :slots, at] = image_ref[:, columns]
                out_ref[member, slots:, :width] = targets
                out_ref[member, slots:, width:] = extra


def embed_kernel(
    own_slots, got_ref, other_ref, text_hbm, rows_ref, out_ref, text_ref, sem
):
    text_copy = pltpu.make_async_copy(text_hbm, text_ref, sem)
    text_copy.start()
    members, tile, chip_width = got_ref.shape
    toks = rows_ref.shape[0]
    width = chip_width // CORES
    core = lax.axis_index("core")
    pl.delay((1 - core) * FIRST_DELAY_NS)
    sources = members // MICRO
    picked = got_ref[pl.ds(core * sources, sources)].reshape(sources * tile, chip_width)
    lanes = picked[:, :128].astype(jnp.float32)
    targets = pltpu.roll(lanes, sources * tile - own_slots, 0)
    row = lax.broadcasted_iota(jnp.int32, lanes.shape, 0)
    col = lax.broadcasted_iota(jnp.int32, lanes.shape, 1).astype(jnp.float32)
    matched = jnp.where(row % tile < own_slots, (targets == col).astype(jnp.float32), 0.0)
    matched = matched.astype(jnp.bfloat16)
    over_rows = (((0,), (0,)), ((), ()))
    placed = lax.dot_general(matched, picked, over_rows, preferred_element_type=jnp.float32)[:toks]
    counts = lax.dot_general(
        matched,
        jnp.ones((sources * tile, width), jnp.bfloat16),
        over_rows,
        preferred_element_type=jnp.float32,
    )[:toks]
    at = pl.ds(pl.multiple_of(core * toks, toks), toks)
    text_copy.wait()
    mine, theirs = text_ref[at, :].astype(jnp.float32), other_ref[at, :].astype(jnp.float32)
    first = core == 0
    for n in range(CORES):
        text = jnp.where(first, mine, theirs) if n == 0 else jnp.where(first, theirs, mine)
        half = slice(n * width, (n + 1) * width)
        rows_ref[:, half] = jnp.where(counts > 0.5, placed[:, half], text).astype(jnp.bfloat16)
    rows = rows_ref[...]
    for i in range(out_ref.shape[0]):
        out_ref[i] = rows


def attend_kernel(tps, head_size, step, *refs):
    @pl.when(lax.axis_index("section") == step)
    def _():
        attend(tps, head_size, *refs)


def attend(
    tps, head_size, rows_ref, gain_ref, query_w, keyval_w, bias_ref, cos_ref, sin_ref, out_ref,
    before=None
):
    chips, toks, chip_width = rows_ref.shape
    width = chip_width // CORES
    features = query_w.shape[0]
    projected = [jnp.zeros((toks, w.shape[1]), jnp.float32) for w in (query_w, keyval_w)]
    squares = jnp.zeros((toks, width), jnp.float32)
    for block in range(chips * CORES):
        if before is not None:
            before(block)
        y, core, x = block // (CORES * tps), block // tps % CORES, block % tps
        gain = gain_ref[block : block + 1, :]
        rows = rows_ref[y * tps + x, :, core * width : (core + 1) * width].astype(jnp.float32)
        squares += rows * rows
        scaled = (rows * gain).astype(jnp.bfloat16)
        at = slice(block * width, (block + 1) * width)
        for n, weight in enumerate((query_w, keyval_w)):
            projected[n] += jnp.dot(scaled, weight[at, :], preferred_element_type=jnp.float32)
    inv_rms = lax.rsqrt(jnp.sum(squares, axis=1, keepdims=True) / features + EPS)
    cosine, sine = cos_ref[...], sin_ref[...]

    def piece(i):
        low = i % 2 * head_size
        return projected[i // 2][:, low : low + head_size] * inv_rms + bias_ref[
            :, i * head_size : (i + 1) * head_size
        ]

    def rotate(values):
        turned = pltpu.roll(values, head_size // 2, 1)
        return (values * cosine + turned * sine).astype(jnp.bfloat16)

    queries = jnp.concatenate([rotate(piece(0)), rotate(piece(1))], axis=0)
    keys = rotate(piece(2))
    values = piece(3).astype(jnp.bfloat16)
    scores = lax.dot_general(
        queries, keys, (((1,), (1,)), ((), ())), preferred_element_type=jnp.float32
    )
    row = lax.broadcasted_iota(jnp.int32, scores.shape, 0) % toks
    col = lax.broadcasted_iota(jnp.int32, scores.shape, 1)
    scores = jnp.where(row >= col, scores / math.sqrt(head_size), -1e30)
    expo = jnp.exp(scores - jnp.max(scores, axis=1, keepdims=True))
    probs = (expo / jnp.sum(expo, axis=1, keepdims=True)).astype(jnp.bfloat16)
    context = jnp.dot(probs, values, preferred_element_type=jnp.float32).astype(jnp.bfloat16)
    context = jnp.concatenate([context[:toks], context[toks:]], axis=1)
    for i in range(chips):
        out_ref[i] = context


def first_attend_kernel(
    tps, head_size, rows_ref, got_ref, bias_ref, cos_ref, sin_ref,
    own_q, other_q, keyval_hbm, out_ref, query_w, keyval_w, gain_out, bias_out, sems
):
    features = query_w.shape[0]
    part = features // LOAD_CHUNKS
    core = lax.axis_index("core")
    chip = lax.axis_index("y") * CORES * tps + lax.axis_index("tp")
    copies = []
    for i in range(LOAD_CHUNKS):
        at = pl.ds(i * part, part)
        own = pl.ds(pl.multiple_of(core * head_size, head_size), head_size)
        other = pl.ds(pl.multiple_of((1 - core) * head_size, head_size), head_size)
        copies.append(
            [
                pltpu.make_async_copy(own_q.at[at], query_w.at[at, own], sems.at[i, 0]),
                pltpu.make_async_copy(other_q.at[at], query_w.at[at, other], sems.at[i, 1]),
                pltpu.make_async_copy(keyval_hbm.at[at], keyval_w.at[at], sems.at[i, 2]),
            ]
        )
    for group in copies:
        for copy in group:
            copy.start()
    blocks = rows_ref.shape[0] * CORES

    def before(block):
        if block % (blocks // LOAD_CHUNKS) == 0:
            for copy in copies[block // (blocks // LOAD_CHUNKS)]:
                copy.wait()

    width = gain_out.shape[1]
    tile = got_ref.shape[1]
    for block in range(blocks):
        gain = got_ref[block, :, width:].astype(jnp.float32)
        gain_out[block : block + 1, :] = gain[tile - 1 :]
    for i in range(CORES):
        own = got_ref[chip + i * tps, :, width : width + head_size].astype(jnp.float32)
        bias_out[:, i * head_size : (i + 1) * head_size] = own[tile // 2 : tile // 2 + 1]
    bias_out[:, CORES * head_size :] = bias_ref[...].astype(jnp.float32)
    active = lax.axis_index("section") == 0

    @pl.when(active)
    def _():
        attend(
            tps, head_size, rows_ref, gain_out, query_w, keyval_w, bias_out, cos_ref, sin_ref,
            out_ref, before=before,
        )

    @pl.when(jnp.logical_not(active))
    def _():
        for block in range(blocks):
            before(block)


def output_kernel(
    tps, step, last, context_ref, own_w, other_w, residual_ref, *refs
):
    out_ref, keep_ref = refs[-2:]
    chips, toks, chip_head = context_ref.shape
    head = chip_head // CORES
    width = own_w.shape[1]
    halves = [slice(n * width, (n + 1) * width) for n in range(CORES)]
    pair = 2 if tps % 2 == 0 else 1
    core_index = lax.axis_index("core")
    first = core_index == 0
    active = lax.axis_index("section") == step

    def keep(kept):
        if last:
            out_ref[...] = jnp.where(first, kept[0], kept[1])
            keep_ref[...] = jnp.where(first, kept[1], kept[0])
        else:
            for at, half in zip(halves, kept):
                keep_ref[:, at] = half

    @pl.when(active)
    def _():
        pl.delay(core_index * STEP_DELAY_NS)
        updates = [jnp.zeros((toks, width), jnp.float32) for _ in range(CORES)]
        for y in range(chips // tps):
            for core in range(CORES):
                for x in range(0, tps, pair):
                    context = jnp.concatenate(
                        [
                            context_ref[y * tps + x + k, :, core * head : (core + 1) * head]
                            for k in range(pair)
                        ],
                        axis=1,
                    )
                    block = (y * CORES + core) * tps + x
                    at = slice(block * head, (block + pair) * head)
                    for n, weight in enumerate((own_w, other_w)):
                        updates[n] += jnp.dot(
                            context, weight[at, :], preferred_element_type=jnp.float32
                        )
        results = []
        for n, at in enumerate(halves):
            update = jnp.where(first, updates[n], updates[1 - n])
            result = (residual_ref[:, at].astype(jnp.float32) + update).astype(jnp.bfloat16)
            results.append(result)
            if not last:
                out_ref[:, at] = result
        keep(results)

    if step > 0:

        @pl.when(jnp.logical_not(active))
        def _():
            keep([refs[0][:, at] for at in halves])


def join_kernel(mine_ref, theirs_ref, out_ref):
    toks = mine_ref.shape[0]
    core = lax.axis_index("core")
    out_ref[pl.ds(pl.multiple_of(core * toks, toks), toks), :] = mine_ref[...]
    out_ref[pl.ds(pl.multiple_of((1 - core) * toks, toks), toks), :] = theirs_ref[...]


def per_device(
    text_rows, image_rows, image_target, norm_gain, q_weight, q_bias, kv_weight, kv_bias, out_weight
):
    plane, chips = ("y", "core", "tp"), ("y", "tp")
    members, chip_count = lax.axis_size(plane), lax.axis_size(chips)
    ys, tps = lax.axis_size("y"), lax.axis_size("tp")
    sections = lax.axis_size("section")
    width = text_rows.shape[1]
    chip_width = CORES * width
    head = q_weight.shape[2]
    features = q_weight.shape[1]
    toks = text_rows.shape[0] // MICRO
    own_slots = image_rows.shape[0]
    sent = vmem_call(
        lambda *refs: pack_kernel(ys, tps, *refs),
        jax.ShapeDtypeStruct((members, 2 * own_slots, chip_width), jnp.bfloat16),
        "pack",
        hbm=(image_target, image_rows, norm_gain, q_bias),
        scratch=[pltpu.SMEM(image_target.shape, jnp.int32)]
        + [pltpu.VMEM(a.shape, a.dtype) for a in (image_rows, norm_gain, q_bias)]
        + [pltpu.SemaphoreType.DMA((4,))],
    )
    got = exchange(sent, plane)
    other_text = swap_cores(text_rows)
    other_q = swap_cores(q_weight[0])
    own_w = out_weight[0]
    other_w = swap_cores(own_w)
    cosine, sine = tables(toks, head)
    got, other_text, other_q, other_w, cosine, sine = lax.optimization_barrier(
        (got, other_text, other_q, other_w, cosine, sine)
    )

    rows = jax.ShapeDtypeStruct((toks, chip_width), jnp.bfloat16)
    text_half = jax.ShapeDtypeStruct((toks, width), jnp.bfloat16)
    copies = jax.ShapeDtypeStruct((chip_count, toks, chip_width), jnp.bfloat16)
    contexts = jax.ShapeDtypeStruct((chip_count, toks, CORES * head), jnp.bfloat16)
    weights = jax.ShapeDtypeStruct((features, CORES * head), jnp.bfloat16)
    current, sent = vmem_call(
        lambda *refs: embed_kernel(own_slots, *refs),
        (rows, copies),
        "embed",
        got, other_text,
        hbm=(text_rows,),
        scratch=[pltpu.VMEM(text_rows.shape, text_rows.dtype), pltpu.SemaphoreType.DMA],
    )
    stored = ()
    for step in range(sections):
        if step > 0:
            order = [(i + step - 1) % sections for i in range(sections)]
            pairs = list(zip(order[::2], order[1::2]))
            route = pairs + [(b, a) for a, b in pairs]
            current = lax.ppermute(current, "section", route)
            sent = jnp.broadcast_to(current[None], copies.shape)
        gathered = exchange(sent, chips)
        if step == 0:
            context, query_w, keyval_w, gain, bias = vmem_call(
                lambda *refs: first_attend_kernel(tps, head, *refs),
                (
                    contexts,
                    weights,
                    weights,
                    jax.ShapeDtypeStruct((members, width), jnp.float32),
                    jax.ShapeDtypeStruct((1, 2 * CORES * head), jnp.float32),
                ),
                "attend_first",
                gathered, got, kv_bias[0], cosine, sine,
                hbm=(q_weight[0], other_q, kv_weight[0, :, 0]),
                scratch=[pltpu.SemaphoreType.DMA((LOAD_CHUNKS, 3))],
            )
        else:
            context = vmem_call(
                lambda *refs: attend_kernel(tps, head, step, *refs),
                contexts,
                "attend",
                gathered, gain, query_w, keyval_w, bias, cosine, sine,
            )
        last = step == sections - 1
        out = text_half if last else rows
        current, keep = vmem_call(
            lambda *refs: output_kernel(tps, step, last, *refs),
            (out, out),
            "output",
            exchange(context, chips), own_w, other_w, current, *stored,
        )
        stored = (keep,)
    joined = jax.ShapeDtypeStruct((MICRO * toks, width), jnp.bfloat16)
    return vmem_call(join_kernel, joined, "join", current, swap_cores(keep))[None]


def solution(mesh):
    sections, seqs, tps = (mesh.shape[name] for name in ("section", "seq", "tp"))
    fine = Mesh(
        mesh.devices.reshape(sections, seqs // CORES, CORES, tps), ("section", "y", "core", "tp")
    )
    seq = ("y", "core")
    in_specs = (
        P(None, (*seq, "tp")),
        P((*seq, "tp"), None),
        P((*seq, "tp")),
        P("section", (*seq, "tp")),
        P("section", None, (*seq, "tp")),
        P("section", (*seq, "tp")),
        P("section", None, "tp", None),
        P("section", "tp", None),
        P("section", None, (*seq, "tp")),
    )
    out_specs = P("section", None, (*seq, "tp"))
    return jax.shard_map(
        per_device, mesh=fine, in_specs=in_specs, out_specs=out_specs, check_vma=False
    )
```

```python
import math

import jax
import jax.numpy as jnp
from jax import lax
from jax.experimental import pallas as pl
from jax.experimental.pallas import tpu as pltpu
from jax.sharding import Mesh
from jax.sharding import PartitionSpec as P

MICRO = 2
CORES = 2
EPS = 1e-06
THETA = 1000000.0
VMEM_LIMIT = 8 * 1024 * 1024
LOAD_CHUNKS = 4
EARLY_CORE = 0
FIRST_DELAY_NS = 5000
STEP_DELAY_NS = 3500


def exchange(blocks, axes):
    return lax.all_to_all(blocks, axes, 0, 0, tiled=True)


def swap_cores(value):
    return lax.ppermute(value, "core", [(0, 1), (1, 0)])


def tables(tok_count, head_size):
    half_size = head_size // 2
    positions = jnp.arange(tok_count, dtype=jnp.float32)
    frequency = THETA ** (-jnp.arange(half_size, dtype=jnp.float32) * 2.0 / head_size)
    angles = positions[:, None] * frequency[None, :]
    cosine = jnp.concatenate([jnp.cos(angles), jnp.cos(angles)], axis=-1)
    sine = jnp.concatenate([-jnp.sin(angles), jnp.sin(angles)], axis=-1)
    return cosine, sine


def vmem_call(kernel, out_shape, name, *args, hbm=(), scratch=(), aliases={}):
    vmem = pl.BlockSpec(memory_space=pltpu.VMEM)
    return pl.pallas_call(
        kernel,
        out_shape=out_shape,
        in_specs=[vmem] * len(args)
        + [pl.BlockSpec(memory_space=pltpu.HBM)] * len(hbm),
        out_specs=jax.tree.map(lambda _: vmem, out_shape),
        scratch_shapes=list(scratch),
        input_output_aliases=aliases,
        compiler_params=pltpu.CompilerParams(vmem_limit_bytes=VMEM_LIMIT),
        name=name,
    )(*args, *(pltpu.with_memory_space_constraint(a, pltpu.HBM) for a in hbm))


def pack_kernel(
    ys, tps, target_hbm, image_hbm, gain_hbm, bias_hbm,
    out_ref, target_ref, image_ref, gain_ref, bias_ref, sems,
):
    copies = [
        pltpu.make_async_copy(src, dst, sems.at[i])
        for i, (src, dst) in enumerate(
            (
                (target_hbm, target_ref),
                (image_hbm, image_ref),
                (gain_hbm, gain_ref),
                (bias_hbm, bias_ref),
            )
        )
    ]
    for copy in copies:
        copy.start()
    slots = image_ref.shape[0]
    width = gain_ref.shape[1]
    head = bias_ref.shape[1]
    at_row = lax.broadcasted_iota(jnp.int32, (slots, width), 0)
    for copy in copies:
        copy.wait()
    targets = jnp.zeros((slots, width), jnp.int32)
    for i in range(slots):
        targets = jnp.where(at_row == i, target_ref[i], targets)
    targets = targets.astype(jnp.float32).astype(jnp.bfloat16)
    bias = jnp.concatenate([bias_ref[...].astype(jnp.float32)] * (width // head), axis=1)
    gain = gain_ref[...].astype(jnp.float32)
    extra = jnp.where(at_row == slots - 1, gain, bias).astype(jnp.bfloat16)
    for y in range(ys):
        for x in range(tps):
            for core in range(CORES):
                member = (y * CORES + core) * tps + x
                for n in range(CORES):
                    at = slice(n * width, (n + 1) * width)
                    block = (y * CORES + n) * tps + x
                    columns = slice(block * width, (block + 1) * width)
                    out_ref[member, :slots, at] = image_ref[:, columns]
                out_ref[member, slots:, :width] = targets
                out_ref[member, slots:, width:] = extra


def embed_kernel(
    own_slots, head_size, got_ref, other_ref, text_hbm, own_q, other_q, keyval_hbm,
    rows_ref, out_ref, query_w, keyval_w, text_ref, sem, sems,
):
    text_copy = pltpu.make_async_copy(text_hbm, text_ref, sem)
    text_copy.start()
    members, tile, chip_width = got_ref.shape
    toks = rows_ref.shape[0]
    width = chip_width // CORES
    core = lax.axis_index("core")
    loads = weight_loads(head_size, own_q, other_q, keyval_hbm, query_w, keyval_w, sems)

    @pl.when(core == EARLY_CORE)
    def _():
        for group in loads:
            for copy in group:
                copy.start()
        pl.delay(FIRST_DELAY_NS)

    sources = members // MICRO
    picked = got_ref[pl.ds(core * sources, sources)].reshape(sources * tile, chip_width)
    lanes = picked[:, :128].astype(jnp.float32)
    targets = pltpu.roll(lanes, sources * tile - own_slots, 0)
    row = lax.broadcasted_iota(jnp.int32, lanes.shape, 0)
    col = lax.broadcasted_iota(jnp.int32, lanes.shape, 1).astype(jnp.float32)
    matched = jnp.where(row % tile < own_slots, (targets == col).astype(jnp.float32), 0.0)
    matched = matched.astype(jnp.bfloat16)
    over_rows = (((0,), (0,)), ((), ()))
    placed = lax.dot_general(matched, picked, over_rows, preferred_element_type=jnp.float32)[:toks]
    counts = lax.dot_general(
        matched,
        jnp.ones((sources * tile, width), jnp.bfloat16),
        over_rows,
        preferred_element_type=jnp.float32,
    )[:toks]
    at = pl.ds(pl.multiple_of(core * toks, toks), toks)
    text_copy.wait()
    mine, theirs = text_ref[at, :].astype(jnp.float32), other_ref[at, :].astype(jnp.float32)
    first = core == 0
    for n in range(CORES):
        text = jnp.where(first, mine, theirs) if n == 0 else jnp.where(first, theirs, mine)
        half = slice(n * width, (n + 1) * width)
        rows_ref[:, half] = jnp.where(counts > 0.5, placed[:, half], text).astype(jnp.bfloat16)
    rows = rows_ref[...]
    for i in range(out_ref.shape[0]):
        out_ref[i] = rows

    @pl.when(core == EARLY_CORE)
    def _():
        for group in loads:
            for copy in group:
                copy.wait()


def attend_kernel(tps, head_size, step, *refs):
    @pl.when(lax.axis_index("section") == step)
    def _():
        attend(tps, head_size, *refs)


def attend(
    tps, head_size, rows_ref, gain_ref, query_w, keyval_w, bias_ref, cos_ref, sin_ref, out_ref,
    before=None
):
    chips, toks, chip_width = rows_ref.shape
    width = chip_width // CORES
    features = query_w.shape[0]
    projected = [jnp.zeros((toks, w.shape[1]), jnp.float32) for w in (query_w, keyval_w)]
    squares = jnp.zeros((toks, width), jnp.float32)
    for block in range(chips * CORES):
        if before is not None:
            before(block)
        y, core, x = block // (CORES * tps), block // tps % CORES, block % tps
        gain = gain_ref[block : block + 1, :]
        rows = rows_ref[y * tps + x, :, core * width : (core + 1) * width].astype(jnp.float32)
        squares += rows * rows
        scaled = (rows * gain).astype(jnp.bfloat16)
        at = slice(block * width, (block + 1) * width)
        for n, weight in enumerate((query_w, keyval_w)):
            projected[n] += jnp.dot(scaled, weight[at, :], preferred_element_type=jnp.float32)
    inv_rms = lax.rsqrt(jnp.sum(squares, axis=1, keepdims=True) / features + EPS)
    cosine, sine = cos_ref[...], sin_ref[...]

    def piece(i):
        low = i % 2 * head_size
        return projected[i // 2][:, low : low + head_size] * inv_rms + bias_ref[
            :, i * head_size : (i + 1) * head_size
        ]

    def rotate(values):
        turned = pltpu.roll(values, head_size // 2, 1)
        return (values * cosine + turned * sine).astype(jnp.bfloat16)

    queries = jnp.concatenate([rotate(piece(0)), rotate(piece(1))], axis=0)
    keys = rotate(piece(2))
    values = piece(3).astype(jnp.bfloat16)
    scores = lax.dot_general(
        queries, keys, (((1,), (1,)), ((), ())), preferred_element_type=jnp.float32
    )
    row = lax.broadcasted_iota(jnp.int32, scores.shape, 0) % toks
    col = lax.broadcasted_iota(jnp.int32, scores.shape, 1)
    scores = jnp.where(row >= col, scores / math.sqrt(head_size), -1e30)
    expo = jnp.exp(scores - jnp.max(scores, axis=1, keepdims=True))
    probs = (expo / jnp.sum(expo, axis=1, keepdims=True)).astype(jnp.bfloat16)
    context = jnp.dot(probs, values, preferred_element_type=jnp.float32).astype(jnp.bfloat16)
    context = jnp.concatenate([context[:toks], context[toks:]], axis=1)
    for i in range(chips):
        out_ref[i] = context


def weight_loads(head_size, own_q, other_q, keyval_hbm, query_w, keyval_w, sems):
    part = query_w.shape[0] // LOAD_CHUNKS
    core = lax.axis_index("core")
    own = pl.ds(pl.multiple_of(core * head_size, head_size), head_size)
    other = pl.ds(pl.multiple_of((1 - core) * head_size, head_size), head_size)
    loads = []
    for i in range(LOAD_CHUNKS):
        at = pl.ds(i * part, part)
        loads.append(
            [
                pltpu.make_async_copy(own_q.at[at], query_w.at[at, own], sems.at[i, 0]),
                pltpu.make_async_copy(other_q.at[at], query_w.at[at, other], sems.at[i, 1]),
                pltpu.make_async_copy(keyval_hbm.at[at], keyval_w.at[at], sems.at[i, 2]),
            ]
        )
    return loads


def first_attend_kernel(
    tps, head_size, rows_ref, got_ref, bias_ref, cos_ref, sin_ref, _query, _keyval,
    own_q, other_q, keyval_hbm, out_ref, query_w, keyval_w, gain_out, bias_out, sems,
):
    chip = lax.axis_index("y") * CORES * tps + lax.axis_index("tp")
    loading = lax.axis_index("core") != EARLY_CORE
    loads = weight_loads(head_size, own_q, other_q, keyval_hbm, query_w, keyval_w, sems)

    @pl.when(loading)
    def _():
        for group in loads:
            for copy in group:
                copy.start()

    blocks = rows_ref.shape[0] * CORES

    def before(block):
        if block % (blocks // LOAD_CHUNKS) == 0:

            @pl.when(loading)
            def _():
                for copy in loads[block // (blocks // LOAD_CHUNKS)]:
                    copy.wait()

    width = gain_out.shape[1]
    tile = got_ref.shape[1]
    for block in range(blocks):
        gain = got_ref[block, :, width:].astype(jnp.float32)
        gain_out[block : block + 1, :] = gain[tile - 1 :]
    for i in range(CORES):
        own = got_ref[chip + i * tps, :, width : width + head_size].astype(jnp.float32)
        bias_out[:, i * head_size : (i + 1) * head_size] = own[tile // 2 : tile // 2 + 1]
    bias_out[:, CORES * head_size :] = bias_ref[...].astype(jnp.float32)
    active = lax.axis_index("section") == 0

    @pl.when(active)
    def _():
        attend(
            tps, head_size, rows_ref, gain_out, query_w, keyval_w, bias_out, cos_ref, sin_ref,
            out_ref, before=before,
        )

    @pl.when(jnp.logical_not(active))
    def _():
        for block in range(blocks):
            before(block)


def output_kernel(
    tps, step, last, context_ref, own_w, other_w, residual_ref, *refs
):
    out_ref, keep_ref = refs[-2:]
    chips, toks, chip_head = context_ref.shape
    head = chip_head // CORES
    width = own_w.shape[1]
    halves = [slice(n * width, (n + 1) * width) for n in range(CORES)]
    pair = 2 if tps % 2 == 0 else 1
    core_index = lax.axis_index("core")
    first = core_index == 0
    active = lax.axis_index("section") == step

    def keep(kept):
        if last:
            out_ref[...] = jnp.where(first, kept[0], kept[1])
            keep_ref[...] = jnp.where(first, kept[1], kept[0])
        else:
            for at, half in zip(halves, kept):
                keep_ref[:, at] = half

    @pl.when(active)
    def _():
        if step > 0:
            pl.delay(core_index * STEP_DELAY_NS)
        updates = [jnp.zeros((toks, width), jnp.float32) for _ in range(CORES)]
        for y in range(chips // tps):
            for core in range(CORES):
                for x in range(0, tps, pair):
                    context = jnp.concatenate(
                        [
                            context_ref[y * tps + x + k, :, core * head : (core + 1) * head]
                            for k in range(pair)
                        ],
                        axis=1,
                    )
                    block = (y * CORES + core) * tps + x
                    at = slice(block * head, (block + pair) * head)
                    for n, weight in enumerate((own_w, other_w)):
                        updates[n] += jnp.dot(
                            context, weight[at, :], preferred_element_type=jnp.float32
                        )
        results = []
        for n, at in enumerate(halves):
            update = jnp.where(first, updates[n], updates[1 - n])
            result = (residual_ref[:, at].astype(jnp.float32) + update).astype(jnp.bfloat16)
            results.append(result)
            if not last:
                out_ref[:, at] = result
        keep(results)

    if step > 0:

        @pl.when(jnp.logical_not(active))
        def _():
            keep([refs[0][:, at] for at in halves])


def join_kernel(mine_ref, theirs_ref, out_ref):
    toks = mine_ref.shape[0]
    core = lax.axis_index("core")
    out_ref[pl.ds(pl.multiple_of(core * toks, toks), toks), :] = mine_ref[...]
    out_ref[pl.ds(pl.multiple_of((1 - core) * toks, toks), toks), :] = theirs_ref[...]


def per_device(
    text_rows, image_rows, image_target, norm_gain, q_weight, q_bias, kv_weight, kv_bias, out_weight
):
    plane, chips = ("y", "core", "tp"), ("y", "tp")
    members, chip_count = lax.axis_size(plane), lax.axis_size(chips)
    ys, tps = lax.axis_size("y"), lax.axis_size("tp")
    sections = lax.axis_size("section")
    width = text_rows.shape[1]
    chip_width = CORES * width
    head = q_weight.shape[2]
    features = q_weight.shape[1]
    toks = text_rows.shape[0] // MICRO
    own_slots = image_rows.shape[0]
    sent = vmem_call(
        lambda *refs: pack_kernel(ys, tps, *refs),
        jax.ShapeDtypeStruct((members, 2 * own_slots, chip_width), jnp.bfloat16),
        "pack",
        hbm=(image_target, image_rows, norm_gain, q_bias),
        scratch=[pltpu.SMEM(image_target.shape, jnp.int32)]
        + [pltpu.VMEM(a.shape, a.dtype) for a in (image_rows, norm_gain, q_bias)]
        + [pltpu.SemaphoreType.DMA((4,))],
    )
    got = exchange(sent, plane)
    other_text = swap_cores(text_rows)
    other_q = swap_cores(q_weight[0])
    own_w = out_weight[0]
    other_w = swap_cores(own_w)
    cosine, sine = tables(toks, head)
    got, other_text, other_q, other_w, cosine, sine = lax.optimization_barrier(
        (got, other_text, other_q, other_w, cosine, sine)
    )

    rows = jax.ShapeDtypeStruct((toks, chip_width), jnp.bfloat16)
    text_half = jax.ShapeDtypeStruct((toks, width), jnp.bfloat16)
    copies = jax.ShapeDtypeStruct((chip_count, toks, chip_width), jnp.bfloat16)
    contexts = jax.ShapeDtypeStruct((chip_count, toks, CORES * head), jnp.bfloat16)
    weights = jax.ShapeDtypeStruct((features, CORES * head), jnp.bfloat16)
    wide = (q_weight[0], other_q, kv_weight[0, :, 0])
    current, sent, query_w, keyval_w = vmem_call(
        lambda *refs: embed_kernel(own_slots, head, *refs),
        (rows, copies, weights, weights),
        "embed",
        got, other_text,
        hbm=(text_rows, *wide),
        scratch=[
            pltpu.VMEM(text_rows.shape, text_rows.dtype),
            pltpu.SemaphoreType.DMA,
            pltpu.SemaphoreType.DMA((LOAD_CHUNKS, 3)),
        ],
    )
    stored = ()
    for step in range(sections):
        if step > 0:
            order = [(i + step - 1) % sections for i in range(sections)]
            pairs = list(zip(order[::2], order[1::2]))
            route = pairs + [(b, a) for a, b in pairs]
            current = lax.ppermute(current, "section", route)
            sent = jnp.broadcast_to(current[None], copies.shape)
        gathered = exchange(sent, chips)
        if step == 0:
            context, query_w, keyval_w, gain, bias = vmem_call(
                lambda *refs: first_attend_kernel(tps, head, *refs),
                (
                    contexts,
                    weights,
                    weights,
                    jax.ShapeDtypeStruct((members, width), jnp.float32),
                    jax.ShapeDtypeStruct((1, 2 * CORES * head), jnp.float32),
                ),
                "attend_first",
                gathered, got, kv_bias[0], cosine, sine, query_w, keyval_w,
                hbm=wide,
                aliases={5: 1, 6: 2},
                scratch=[pltpu.SemaphoreType.DMA((LOAD_CHUNKS, 3))],
            )
        else:
            context = vmem_call(
                lambda *refs: attend_kernel(tps, head, step, *refs),
                contexts,
                "attend",
                gathered, gain, query_w, keyval_w, bias, cosine, sine,
            )
        last = step == sections - 1
        out = text_half if last else rows
        current, keep = vmem_call(
            lambda *refs: output_kernel(tps, step, last, *refs),
            (out, out),
            "output",
            exchange(context, chips), own_w, other_w, current, *stored,
        )
        stored = (keep,)
    joined = jax.ShapeDtypeStruct((MICRO * toks, width), jnp.bfloat16)
    return vmem_call(join_kernel, joined, "join", current, swap_cores(keep))[None]


def solution(mesh):
    sections, seqs, tps = (mesh.shape[name] for name in ("section", "seq", "tp"))
    fine = Mesh(
        mesh.devices.reshape(sections, seqs // CORES, CORES, tps), ("section", "y", "core", "tp")
    )
    seq = ("y", "core")
    in_specs = (
        P(None, (*seq, "tp")),
        P((*seq, "tp"), None),
        P((*seq, "tp")),
        P("section", (*seq, "tp")),
        P("section", None, (*seq, "tp")),
        P("section", (*seq, "tp")),
        P("section", None, "tp", None),
        P("section", "tp", None),
        P("section", None, (*seq, "tp")),
    )
    out_specs = P("section", None, (*seq, "tp"))
    return jax.shard_map(
        per_device, mesh=fine, in_specs=in_specs, out_specs=out_specs, check_vma=False
    )
```

```python
import math

import jax
import jax.numpy as jnp
from jax import lax
from jax.experimental import pallas as pl
from jax.experimental.pallas import tpu as pltpu
from jax.sharding import Mesh
from jax.sharding import PartitionSpec as P

MICRO = 2
CORES = 2
EPS = 1e-06
THETA = 1000000.0
VMEM_LIMIT = 8 * 1024 * 1024
LOAD_CHUNKS = 4
EARLY_CORE = 0
FIRST_DELAY_NS = 4500
STEP_DELAY_NS = 3500


def exchange(blocks, axes):
    return lax.all_to_all(blocks, axes, 0, 0, tiled=True)


def swap_cores(value):
    return lax.ppermute(value, "core", [(0, 1), (1, 0)])


def tables(tok_count, head_size):
    half_size = head_size // 2
    positions = jnp.arange(tok_count, dtype=jnp.float32)
    frequency = THETA ** (-jnp.arange(half_size, dtype=jnp.float32) * 2.0 / head_size)
    angles = positions[:, None] * frequency[None, :]
    cosine = jnp.concatenate([jnp.cos(angles), jnp.cos(angles)], axis=-1)
    sine = jnp.concatenate([-jnp.sin(angles), jnp.sin(angles)], axis=-1)
    return cosine, sine


def vmem_call(kernel, out_shape, name, *args, hbm=(), scratch=(), aliases={}):
    vmem = pl.BlockSpec(memory_space=pltpu.VMEM)
    return pl.pallas_call(
        kernel,
        out_shape=out_shape,
        in_specs=[vmem] * len(args)
        + [pl.BlockSpec(memory_space=pltpu.HBM)] * len(hbm),
        out_specs=jax.tree.map(lambda _: vmem, out_shape),
        scratch_shapes=list(scratch),
        input_output_aliases=aliases,
        compiler_params=pltpu.CompilerParams(vmem_limit_bytes=VMEM_LIMIT),
        name=name,
    )(*args, *(pltpu.with_memory_space_constraint(a, pltpu.HBM) for a in hbm))


def pack_kernel(
    ys, tps, target_hbm, image_hbm, gain_hbm, bias_hbm,
    out_ref, target_ref, image_ref, gain_ref, bias_ref, sems,
):
    copies = [
        pltpu.make_async_copy(src, dst, sems.at[i])
        for i, (src, dst) in enumerate(
            (
                (target_hbm, target_ref),
                (image_hbm, image_ref),
                (gain_hbm, gain_ref),
                (bias_hbm, bias_ref),
            )
        )
    ]
    for copy in copies:
        copy.start()
    slots = image_ref.shape[0]
    width = gain_ref.shape[1]
    head = bias_ref.shape[1]
    at_row = lax.broadcasted_iota(jnp.int32, (slots, width), 0)
    for copy in copies:
        copy.wait()
    targets = jnp.zeros((slots, width), jnp.int32)
    for i in range(slots):
        targets = jnp.where(at_row == i, target_ref[i], targets)
    targets = targets.astype(jnp.float32).astype(jnp.bfloat16)
    bias = jnp.concatenate([bias_ref[...].astype(jnp.float32)] * (width // head), axis=1)
    gain = gain_ref[...].astype(jnp.float32)
    extra = jnp.where(at_row == slots - 1, gain, bias).astype(jnp.bfloat16)
    for y in range(ys):
        for x in range(tps):
            for core in range(CORES):
                member = (y * CORES + core) * tps + x
                for n in range(CORES):
                    at = slice(n * width, (n + 1) * width)
                    block = (y * CORES + n) * tps + x
                    columns = slice(block * width, (block + 1) * width)
                    out_ref[member, :slots, at] = image_ref[:, columns]
                out_ref[member, slots:, :width] = targets
                out_ref[member, slots:, width:] = extra


def embed_kernel(
    own_slots, head_size, got_ref, other_ref, text_hbm, own_q, other_q, keyval_hbm,
    rows_ref, out_ref, query_w, keyval_w, text_ref, sem, sems,
):
    text_copy = pltpu.make_async_copy(text_hbm, text_ref, sem)
    text_copy.start()
    members, tile, chip_width = got_ref.shape
    toks = rows_ref.shape[0]
    width = chip_width // CORES
    core = lax.axis_index("core")
    loads = weight_loads(head_size, own_q, other_q, keyval_hbm, query_w, keyval_w, sems)

    @pl.when(core == EARLY_CORE)
    def _():
        for group in loads:
            for copy in group:
                copy.start()
        pl.delay(FIRST_DELAY_NS)

    sources = members // MICRO
    picked = got_ref[pl.ds(core * sources, sources)].reshape(sources * tile, chip_width)
    lanes = picked[:, :128].astype(jnp.float32)
    targets = pltpu.roll(lanes, sources * tile - own_slots, 0)
    row = lax.broadcasted_iota(jnp.int32, lanes.shape, 0)
    col = lax.broadcasted_iota(jnp.int32, lanes.shape, 1).astype(jnp.float32)
    matched = jnp.where(row % tile < own_slots, (targets == col).astype(jnp.float32), 0.0)
    matched = matched.astype(jnp.bfloat16)
    over_rows = (((0,), (0,)), ((), ()))
    placed = lax.dot_general(matched, picked, over_rows, preferred_element_type=jnp.float32)[:toks]
    counts = lax.dot_general(
        matched,
        jnp.ones((sources * tile, width), jnp.bfloat16),
        over_rows,
        preferred_element_type=jnp.float32,
    )[:toks]
    at = pl.ds(pl.multiple_of(core * toks, toks), toks)
    text_copy.wait()
    mine, theirs = text_ref[at, :].astype(jnp.float32), other_ref[at, :].astype(jnp.float32)
    first = core == 0
    for n in range(CORES):
        text = jnp.where(first, mine, theirs) if n == 0 else jnp.where(first, theirs, mine)
        half = slice(n * width, (n + 1) * width)
        rows_ref[:, half] = jnp.where(counts > 0.5, placed[:, half], text).astype(jnp.bfloat16)
    rows = rows_ref[...]
    for i in range(out_ref.shape[0]):
        out_ref[i] = rows

    @pl.when(core == EARLY_CORE)
    def _():
        for group in loads:
            for copy in group:
                copy.wait()


def attend_kernel(tps, head_size, step, *refs):
    @pl.when(lax.axis_index("section") == step)
    def _():
        attend(tps, head_size, *refs)


def attend(
    tps, head_size, rows_ref, gain_ref, query_w, keyval_w, bias_ref, cos_ref, sin_ref, out_ref,
    before=None
):
    chips, toks, chip_width = rows_ref.shape
    width = chip_width // CORES
    features = query_w.shape[0]
    projected = [jnp.zeros((toks, w.shape[1]), jnp.float32) for w in (query_w, keyval_w)]
    squares = jnp.zeros((toks, width), jnp.float32)
    for block in range(chips * CORES):
        if before is not None:
            before(block)
        y, core, x = block // (CORES * tps), block // tps % CORES, block % tps
        gain = gain_ref[block : block + 1, :]
        rows = rows_ref[y * tps + x, :, core * width : (core + 1) * width].astype(jnp.float32)
        squares += rows * rows
        scaled = (rows * gain).astype(jnp.bfloat16)
        at = slice(block * width, (block + 1) * width)
        for n, weight in enumerate((query_w, keyval_w)):
            projected[n] += jnp.dot(scaled, weight[at, :], preferred_element_type=jnp.float32)
    inv_rms = lax.rsqrt(jnp.sum(squares, axis=1, keepdims=True) / features + EPS)
    cosine, sine = cos_ref[...], sin_ref[...]

    def piece(i):
        low = i % 2 * head_size
        return projected[i // 2][:, low : low + head_size] * inv_rms + bias_ref[
            :, i * head_size : (i + 1) * head_size
        ]

    def rotate(values):
        turned = pltpu.roll(values, head_size // 2, 1)
        return (values * cosine + turned * sine).astype(jnp.bfloat16)

    queries = jnp.concatenate([rotate(piece(0)), rotate(piece(1))], axis=0)
    keys = rotate(piece(2))
    values = piece(3).astype(jnp.bfloat16)
    scores = lax.dot_general(
        queries, keys, (((1,), (1,)), ((), ())), preferred_element_type=jnp.float32
    )
    row = lax.broadcasted_iota(jnp.int32, scores.shape, 0) % toks
    col = lax.broadcasted_iota(jnp.int32, scores.shape, 1)
    scores = jnp.where(row >= col, scores / math.sqrt(head_size), -1e30)
    expo = jnp.exp(scores - jnp.max(scores, axis=1, keepdims=True))
    probs = (expo / jnp.sum(expo, axis=1, keepdims=True)).astype(jnp.bfloat16)
    context = jnp.dot(probs, values, preferred_element_type=jnp.float32).astype(jnp.bfloat16)
    context = jnp.concatenate([context[:toks], context[toks:]], axis=1)
    for i in range(chips):
        out_ref[i] = context


def weight_loads(head_size, own_q, other_q, keyval_hbm, query_w, keyval_w, sems):
    part = query_w.shape[0] // LOAD_CHUNKS
    core = lax.axis_index("core")
    own = pl.ds(pl.multiple_of(core * head_size, head_size), head_size)
    other = pl.ds(pl.multiple_of((1 - core) * head_size, head_size), head_size)
    loads = []
    for i in range(LOAD_CHUNKS):
        at = pl.ds(i * part, part)
        loads.append(
            [
                pltpu.make_async_copy(own_q.at[at], query_w.at[at, own], sems.at[i, 0]),
                pltpu.make_async_copy(other_q.at[at], query_w.at[at, other], sems.at[i, 1]),
                pltpu.make_async_copy(keyval_hbm.at[at], keyval_w.at[at], sems.at[i, 2]),
            ]
        )
    return loads


def first_attend_kernel(
    tps, head_size, rows_ref, got_ref, bias_ref, cos_ref, sin_ref, _query, _keyval,
    own_q, other_q, keyval_hbm, out_ref, query_w, keyval_w, gain_out, bias_out, sems,
):
    chip = lax.axis_index("y") * CORES * tps + lax.axis_index("tp")
    loading = lax.axis_index("core") != EARLY_CORE
    loads = weight_loads(head_size, own_q, other_q, keyval_hbm, query_w, keyval_w, sems)

    @pl.when(loading)
    def _():
        for group in loads:
            for copy in group:
                copy.start()

    blocks = rows_ref.shape[0] * CORES

    def before(block):
        if block % (blocks // LOAD_CHUNKS) == 0:

            @pl.when(loading)
            def _():
                for copy in loads[block // (blocks // LOAD_CHUNKS)]:
                    copy.wait()

    width = gain_out.shape[1]
    tile = got_ref.shape[1]
    for block in range(blocks):
        gain = got_ref[block, :, width:].astype(jnp.float32)
        gain_out[block : block + 1, :] = gain[tile - 1 :]
    for i in range(CORES):
        own = got_ref[chip + i * tps, :, width : width + head_size].astype(jnp.float32)
        bias_out[:, i * head_size : (i + 1) * head_size] = own[tile // 2 : tile // 2 + 1]
    bias_out[:, CORES * head_size :] = bias_ref[...].astype(jnp.float32)
    active = lax.axis_index("section") == 0

    @pl.when(active)
    def _():
        attend(
            tps, head_size, rows_ref, gain_out, query_w, keyval_w, bias_out, cos_ref, sin_ref,
            out_ref, before=before,
        )

    @pl.when(jnp.logical_not(active))
    def _():
        for block in range(blocks):
            before(block)


def output_kernel(
    tps, step, last, context_ref, own_w, other_w, residual_ref, *refs
):
    out_ref, keep_ref = refs[-2:]
    chips, toks, chip_head = context_ref.shape
    head = chip_head // CORES
    width = own_w.shape[1]
    halves = [slice(n * width, (n + 1) * width) for n in range(CORES)]
    pair = 2 if tps % 2 == 0 else 1
    core_index = lax.axis_index("core")
    first = core_index == 0
    active = lax.axis_index("section") == step

    def keep(kept):
        if last:
            out_ref[...] = jnp.where(first, kept[0], kept[1])
            keep_ref[...] = jnp.where(first, kept[1], kept[0])
        else:
            for at, half in zip(halves, kept):
                keep_ref[:, at] = half

    @pl.when(active)
    def _():
        if step > 0:
            pl.delay(core_index * STEP_DELAY_NS)
        updates = [jnp.zeros((toks, width), jnp.float32) for _ in range(CORES)]
        for y in range(chips // tps):
            for core in range(CORES):
                for x in range(0, tps, pair):
                    context = jnp.concatenate(
                        [
                            context_ref[y * tps + x + k, :, core * head : (core + 1) * head]
                            for k in range(pair)
                        ],
                        axis=1,
                    )
                    block = (y * CORES + core) * tps + x
                    at = slice(block * head, (block + pair) * head)
                    for n, weight in enumerate((own_w, other_w)):
                        updates[n] += jnp.dot(
                            context, weight[at, :], preferred_element_type=jnp.float32
                        )
        results = []
        for n, at in enumerate(halves):
            update = jnp.where(first, updates[n], updates[1 - n])
            result = (residual_ref[:, at].astype(jnp.float32) + update).astype(jnp.bfloat16)
            results.append(result)
            if not last:
                out_ref[:, at] = result
        keep(results)

    if step > 0:

        @pl.when(jnp.logical_not(active))
        def _():
            keep([refs[0][:, at] for at in halves])


def join_kernel(mine_ref, theirs_ref, out_ref):
    toks = mine_ref.shape[0]
    core = lax.axis_index("core")
    out_ref[pl.ds(pl.multiple_of(core * toks, toks), toks), :] = mine_ref[...]
    out_ref[pl.ds(pl.multiple_of((1 - core) * toks, toks), toks), :] = theirs_ref[...]


def per_device(
    text_rows, image_rows, image_target, norm_gain, q_weight, q_bias, kv_weight, kv_bias, out_weight
):
    plane, chips = ("y", "core", "tp"), ("y", "tp")
    members, chip_count = lax.axis_size(plane), lax.axis_size(chips)
    ys, tps = lax.axis_size("y"), lax.axis_size("tp")
    sections = lax.axis_size("section")
    width = text_rows.shape[1]
    chip_width = CORES * width
    head = q_weight.shape[2]
    features = q_weight.shape[1]
    toks = text_rows.shape[0] // MICRO
    own_slots = image_rows.shape[0]
    sent = vmem_call(
        lambda *refs: pack_kernel(ys, tps, *refs),
        jax.ShapeDtypeStruct((members, 2 * own_slots, chip_width), jnp.bfloat16),
        "pack",
        hbm=(image_target, image_rows, norm_gain, q_bias),
        scratch=[pltpu.SMEM(image_target.shape, jnp.int32)]
        + [pltpu.VMEM(a.shape, a.dtype) for a in (image_rows, norm_gain, q_bias)]
        + [pltpu.SemaphoreType.DMA((4,))],
    )
    sent, text_sent, q_sent, w_sent = lax.optimization_barrier(
        (sent, text_rows, q_weight[0], out_weight[0])
    )
    got = exchange(sent, plane)
    other_text = swap_cores(text_sent)
    other_q = swap_cores(q_sent)
    own_w = out_weight[0]
    other_w = swap_cores(w_sent)
    cosine, sine = tables(toks, head)
    got, other_text, other_q, other_w, cosine, sine = lax.optimization_barrier(
        (got, other_text, other_q, other_w, cosine, sine)
    )

    rows = jax.ShapeDtypeStruct((toks, chip_width), jnp.bfloat16)
    text_half = jax.ShapeDtypeStruct((toks, width), jnp.bfloat16)
    copies = jax.ShapeDtypeStruct((chip_count, toks, chip_width), jnp.bfloat16)
    contexts = jax.ShapeDtypeStruct((chip_count, toks, CORES * head), jnp.bfloat16)
    weights = jax.ShapeDtypeStruct((features, CORES * head), jnp.bfloat16)
    wide = (q_weight[0], other_q, kv_weight[0, :, 0])
    current, sent, query_w, keyval_w = vmem_call(
        lambda *refs: embed_kernel(own_slots, head, *refs),
        (rows, copies, weights, weights),
        "embed",
        got, other_text,
        hbm=(text_rows, *wide),
        scratch=[
            pltpu.VMEM(text_rows.shape, text_rows.dtype),
            pltpu.SemaphoreType.DMA,
            pltpu.SemaphoreType.DMA((LOAD_CHUNKS, 3)),
        ],
    )
    stored = ()
    for step in range(sections):
        if step > 0:
            order = [(i + step - 1) % sections for i in range(sections)]
            pairs = list(zip(order[::2], order[1::2]))
            route = pairs + [(b, a) for a, b in pairs]
            current = lax.ppermute(current, "section", route)
            sent = jnp.broadcast_to(current[None], copies.shape)
        gathered = exchange(sent, chips)
        if step == 0:
            context, query_w, keyval_w, gain, bias = vmem_call(
                lambda *refs: first_attend_kernel(tps, head, *refs),
                (
                    contexts,
                    weights,
                    weights,
                    jax.ShapeDtypeStruct((members, width), jnp.float32),
                    jax.ShapeDtypeStruct((1, 2 * CORES * head), jnp.float32),
                ),
                "attend_first",
                gathered, got, kv_bias[0], cosine, sine, query_w, keyval_w,
                hbm=wide,
                aliases={5: 1, 6: 2},
                scratch=[pltpu.SemaphoreType.DMA((LOAD_CHUNKS, 3))],
            )
        else:
            context = vmem_call(
                lambda *refs: attend_kernel(tps, head, step, *refs),
                contexts,
                "attend",
                gathered, gain, query_w, keyval_w, bias, cosine, sine,
            )
        last = step == sections - 1
        out = text_half if last else rows
        current, keep = vmem_call(
            lambda *refs: output_kernel(tps, step, last, *refs),
            (out, out),
            "output",
            exchange(context, chips), own_w, other_w, current, *stored,
        )
        stored = (keep,)
    joined = jax.ShapeDtypeStruct((MICRO * toks, width), jnp.bfloat16)
    return vmem_call(join_kernel, joined, "join", current, swap_cores(keep))[None]


def solution(mesh):
    sections, seqs, tps = (mesh.shape[name] for name in ("section", "seq", "tp"))
    fine = Mesh(
        mesh.devices.reshape(sections, seqs // CORES, CORES, tps), ("section", "y", "core", "tp")
    )
    seq = ("y", "core")
    in_specs = (
        P(None, (*seq, "tp")),
        P((*seq, "tp"), None),
        P((*seq, "tp")),
        P("section", (*seq, "tp")),
        P("section", None, (*seq, "tp")),
        P("section", (*seq, "tp")),
        P("section", None, "tp", None),
        P("section", "tp", None),
        P("section", None, (*seq, "tp")),
    )
    out_specs = P("section", None, (*seq, "tp"))
    return jax.shard_map(
        per_device, mesh=fine, in_specs=in_specs, out_specs=out_specs, check_vma=False
    )
```

```python
import math

import jax
import jax.numpy as jnp
from jax import lax
from jax.experimental import pallas as pl
from jax.experimental.pallas import tpu as pltpu
from jax.sharding import Mesh
from jax.sharding import PartitionSpec as P

MICRO = 2
CORES = 2
EPS = 1e-06
THETA = 1000000.0
VMEM_LIMIT = 8 * 1024 * 1024
LOAD_CHUNKS = 4
EARLY_CORE = 0
FIRST_DELAY_NS = 4000
STEP_DELAY_NS = 3500


def exchange(blocks, axes):
    return lax.all_to_all(blocks, axes, 0, 0, tiled=True)


def swap_cores(value):
    return lax.ppermute(value, "core", [(0, 1), (1, 0)])


def tables(tok_count, head_size):
    half_size = head_size // 2
    positions = jnp.arange(tok_count, dtype=jnp.float32)
    frequency = THETA ** (-jnp.arange(half_size, dtype=jnp.float32) * 2.0 / head_size)
    angles = positions[:, None] * frequency[None, :]
    cosine = jnp.concatenate([jnp.cos(angles), jnp.cos(angles)], axis=-1)
    sine = jnp.concatenate([-jnp.sin(angles), jnp.sin(angles)], axis=-1)
    return cosine, sine


def vmem_call(kernel, out_shape, name, *args, hbm=(), scratch=(), aliases={}):
    vmem = pl.BlockSpec(memory_space=pltpu.VMEM)
    return pl.pallas_call(
        kernel,
        out_shape=out_shape,
        in_specs=[vmem] * len(args)
        + [pl.BlockSpec(memory_space=pltpu.HBM)] * len(hbm),
        out_specs=jax.tree.map(lambda _: vmem, out_shape),
        scratch_shapes=list(scratch),
        input_output_aliases=aliases,
        compiler_params=pltpu.CompilerParams(vmem_limit_bytes=VMEM_LIMIT),
        name=name,
    )(*args, *(pltpu.with_memory_space_constraint(a, pltpu.HBM) for a in hbm))


def pack_kernel(
    ys, tps, target_hbm, image_hbm, gain_hbm, bias_hbm,
    out_ref, target_ref, image_ref, gain_ref, bias_ref, sems,
):
    copies = [
        pltpu.make_async_copy(src, dst, sems.at[i])
        for i, (src, dst) in enumerate(
            (
                (target_hbm, target_ref),
                (image_hbm, image_ref),
                (gain_hbm, gain_ref),
                (bias_hbm, bias_ref),
            )
        )
    ]
    for copy in copies:
        copy.start()
    slots = image_ref.shape[0]
    width = gain_ref.shape[1]
    head = bias_ref.shape[1]
    at_row = lax.broadcasted_iota(jnp.int32, (slots, width), 0)
    for copy in copies:
        copy.wait()
    targets = jnp.zeros((slots, width), jnp.int32)
    for i in range(slots):
        targets = jnp.where(at_row == i, target_ref[i], targets)
    targets = targets.astype(jnp.float32).astype(jnp.bfloat16)
    bias = jnp.concatenate([bias_ref[...].astype(jnp.float32)] * (width // head), axis=1)
    gain = gain_ref[...].astype(jnp.float32)
    extra = jnp.where(at_row == slots - 1, gain, bias).astype(jnp.bfloat16)
    for y in range(ys):
        for x in range(tps):
            for core in range(CORES):
                member = (y * CORES + core) * tps + x
                for n in range(CORES):
                    at = slice(n * width, (n + 1) * width)
                    block = (y * CORES + n) * tps + x
                    columns = slice(block * width, (block + 1) * width)
                    out_ref[member, :slots, at] = image_ref[:, columns]
                out_ref[member, slots:, :width] = targets
                out_ref[member, slots:, width:] = extra


def embed_kernel(
    own_slots, head_size, got_ref, other_ref, text_hbm, own_q, other_q, keyval_hbm,
    rows_ref, out_ref, query_w, keyval_w, text_ref, sem, sems,
):
    text_copy = pltpu.make_async_copy(text_hbm, text_ref, sem)
    text_copy.start()
    members, tile, chip_width = got_ref.shape
    toks = rows_ref.shape[0]
    width = chip_width // CORES
    core = lax.axis_index("core")
    loads = weight_loads(head_size, own_q, other_q, keyval_hbm, query_w, keyval_w, sems)

    @pl.when(core == EARLY_CORE)
    def _():
        for group in loads:
            for copy in group:
                copy.start()
        pl.delay(FIRST_DELAY_NS)

    sources = members // MICRO
    picked = got_ref[pl.ds(core * sources, sources)].reshape(sources * tile, chip_width)
    lanes = picked[:, :128].astype(jnp.float32)
    targets = pltpu.roll(lanes, sources * tile - own_slots, 0)
    row = lax.broadcasted_iota(jnp.int32, lanes.shape, 0)
    col = lax.broadcasted_iota(jnp.int32, lanes.shape, 1).astype(jnp.float32)
    matched = jnp.where(row % tile < own_slots, (targets == col).astype(jnp.float32), 0.0)
    matched = matched.astype(jnp.bfloat16)
    over_rows = (((0,), (0,)), ((), ()))
    placed = lax.dot_general(matched, picked, over_rows, preferred_element_type=jnp.float32)[:toks]
    counts = lax.dot_general(
        matched,
        jnp.ones((sources * tile, width), jnp.bfloat16),
        over_rows,
        preferred_element_type=jnp.float32,
    )[:toks]
    at = pl.ds(pl.multiple_of(core * toks, toks), toks)
    text_copy.wait()
    mine, theirs = text_ref[at, :].astype(jnp.float32), other_ref[at, :].astype(jnp.float32)
    first = core == 0
    for n in range(CORES):
        text = jnp.where(first, mine, theirs) if n == 0 else jnp.where(first, theirs, mine)
        half = slice(n * width, (n + 1) * width)
        rows_ref[:, half] = jnp.where(counts > 0.5, placed[:, half], text).astype(jnp.bfloat16)
    rows = rows_ref[...]
    for i in range(out_ref.shape[0]):
        out_ref[i] = rows

    @pl.when(core == EARLY_CORE)
    def _():
        for group in loads:
            for copy in group:
                copy.wait()


def attend_kernel(tps, head_size, step, *refs):
    @pl.when(lax.axis_index("section") == step)
    def _():
        attend(tps, head_size, *refs)


def attend(
    tps, head_size, rows_ref, gain_ref, query_w, keyval_w, bias_ref, cos_ref, sin_ref, out_ref,
    before=None
):
    chips, toks, chip_width = rows_ref.shape
    width = chip_width // CORES
    features = query_w.shape[0]
    projected = [jnp.zeros((toks, w.shape[1]), jnp.float32) for w in (query_w, keyval_w)]
    squares = jnp.zeros((toks, width), jnp.float32)
    for block in range(chips * CORES):
        if before is not None:
            before(block)
        y, core, x = block // (CORES * tps), block // tps % CORES, block % tps
        gain = gain_ref[block : block + 1, :]
        rows = rows_ref[y * tps + x, :, core * width : (core + 1) * width].astype(jnp.float32)
        squares += rows * rows
        scaled = (rows * gain).astype(jnp.bfloat16)
        at = slice(block * width, (block + 1) * width)
        for n, weight in enumerate((query_w, keyval_w)):
            projected[n] += jnp.dot(scaled, weight[at, :], preferred_element_type=jnp.float32)
    inv_rms = lax.rsqrt(jnp.sum(squares, axis=1, keepdims=True) / features + EPS)
    cosine, sine = cos_ref[...], sin_ref[...]

    def piece(i):
        low = i % 2 * head_size
        return projected[i // 2][:, low : low + head_size] * inv_rms + bias_ref[
            :, i * head_size : (i + 1) * head_size
        ]

    def rotate(values):
        turned = pltpu.roll(values, head_size // 2, 1)
        return (values * cosine + turned * sine).astype(jnp.bfloat16)

    queries = jnp.concatenate([rotate(piece(0)), rotate(piece(1))], axis=0)
    keys = rotate(piece(2))
    values = piece(3).astype(jnp.bfloat16)
    scores = lax.dot_general(
        queries, keys, (((1,), (1,)), ((), ())), preferred_element_type=jnp.float32
    )
    row = lax.broadcasted_iota(jnp.int32, scores.shape, 0) % toks
    col = lax.broadcasted_iota(jnp.int32, scores.shape, 1)
    scores = jnp.where(row >= col, scores / math.sqrt(head_size), -1e30)
    expo = jnp.exp(scores - jnp.max(scores, axis=1, keepdims=True))
    probs = (expo / jnp.sum(expo, axis=1, keepdims=True)).astype(jnp.bfloat16)
    context = jnp.dot(probs, values, preferred_element_type=jnp.float32).astype(jnp.bfloat16)
    context = jnp.concatenate([context[:toks], context[toks:]], axis=1)
    for i in range(chips):
        out_ref[i] = context


def weight_loads(head_size, own_q, other_q, keyval_hbm, query_w, keyval_w, sems):
    part = query_w.shape[0] // LOAD_CHUNKS
    core = lax.axis_index("core")
    own = pl.ds(pl.multiple_of(core * head_size, head_size), head_size)
    other = pl.ds(pl.multiple_of((1 - core) * head_size, head_size), head_size)
    loads = []
    for i in range(LOAD_CHUNKS):
        at = pl.ds(i * part, part)
        loads.append(
            [
                pltpu.make_async_copy(own_q.at[at], query_w.at[at, own], sems.at[i, 0]),
                pltpu.make_async_copy(other_q.at[at], query_w.at[at, other], sems.at[i, 1]),
                pltpu.make_async_copy(keyval_hbm.at[at], keyval_w.at[at], sems.at[i, 2]),
            ]
        )
    return loads


def first_attend_kernel(
    tps, head_size, rows_ref, got_ref, bias_ref, cos_ref, sin_ref, _query, _keyval,
    own_q, other_q, keyval_hbm, out_ref, query_w, keyval_w, gain_out, bias_out, sems,
):
    chip = lax.axis_index("y") * CORES * tps + lax.axis_index("tp")
    loading = lax.axis_index("core") != EARLY_CORE
    loads = weight_loads(head_size, own_q, other_q, keyval_hbm, query_w, keyval_w, sems)

    @pl.when(loading)
    def _():
        for group in loads:
            for copy in group:
                copy.start()

    blocks = rows_ref.shape[0] * CORES

    def before(block):
        if block % (blocks // LOAD_CHUNKS) == 0:

            @pl.when(loading)
            def _():
                for copy in loads[block // (blocks // LOAD_CHUNKS)]:
                    copy.wait()

    width = gain_out.shape[1]
    tile = got_ref.shape[1]
    for block in range(blocks):
        gain = got_ref[block, :, width:].astype(jnp.float32)
        gain_out[block : block + 1, :] = gain[tile - 1 :]
    for i in range(CORES):
        own = got_ref[chip + i * tps, :, width : width + head_size].astype(jnp.float32)
        bias_out[:, i * head_size : (i + 1) * head_size] = own[tile // 2 : tile // 2 + 1]
    bias_out[:, CORES * head_size :] = bias_ref[...].astype(jnp.float32)
    active = lax.axis_index("section") == 0

    @pl.when(active)
    def _():
        attend(
            tps, head_size, rows_ref, gain_out, query_w, keyval_w, bias_out, cos_ref, sin_ref,
            out_ref, before=before,
        )

    @pl.when(jnp.logical_not(active))
    def _():
        for block in range(blocks):
            before(block)


def output_kernel(
    tps, step, last, context_ref, own_w, other_w, residual_ref, *refs
):
    out_ref, keep_ref = refs[-2:]
    chips, toks, chip_head = context_ref.shape
    head = chip_head // CORES
    width = own_w.shape[1]
    halves = [slice(n * width, (n + 1) * width) for n in range(CORES)]
    pair = 2 if tps % 2 == 0 else 1
    core_index = lax.axis_index("core")
    first = core_index == 0
    active = lax.axis_index("section") == step

    def keep(kept):
        if last:
            out_ref[...] = jnp.where(first, kept[0], kept[1])
            keep_ref[...] = jnp.where(first, kept[1], kept[0])
        else:
            for at, half in zip(halves, kept):
                keep_ref[:, at] = half

    @pl.when(active)
    def _():
        if step > 0:
            pl.delay(core_index * STEP_DELAY_NS)
        updates = [jnp.zeros((toks, width), jnp.float32) for _ in range(CORES)]
        for y in range(chips // tps):
            for core in range(CORES):
                for x in range(0, tps, pair):
                    context = jnp.concatenate(
                        [
                            context_ref[y * tps + x + k, :, core * head : (core + 1) * head]
                            for k in range(pair)
                        ],
                        axis=1,
                    )
                    block = (y * CORES + core) * tps + x
                    at = slice(block * head, (block + pair) * head)
                    for n, weight in enumerate((own_w, other_w)):
                        updates[n] += jnp.dot(
                            context, weight[at, :], preferred_element_type=jnp.float32
                        )
        results = []
        for n, at in enumerate(halves):
            update = jnp.where(first, updates[n], updates[1 - n])
            result = (residual_ref[:, at].astype(jnp.float32) + update).astype(jnp.bfloat16)
            results.append(result)
            if not last:
                out_ref[:, at] = result
        keep(results)

    if step > 0:

        @pl.when(jnp.logical_not(active))
        def _():
            keep([refs[0][:, at] for at in halves])


def join_kernel(mine_ref, theirs_ref, out_ref):
    toks = mine_ref.shape[0]
    core = lax.axis_index("core")
    out_ref[pl.ds(pl.multiple_of(core * toks, toks), toks), :] = mine_ref[...]
    out_ref[pl.ds(pl.multiple_of((1 - core) * toks, toks), toks), :] = theirs_ref[...]


def per_device(
    text_rows, image_rows, image_target, norm_gain, q_weight, q_bias, kv_weight, kv_bias, out_weight
):
    plane, chips = ("y", "core", "tp"), ("y", "tp")
    members, chip_count = lax.axis_size(plane), lax.axis_size(chips)
    ys, tps = lax.axis_size("y"), lax.axis_size("tp")
    sections = lax.axis_size("section")
    width = text_rows.shape[1]
    chip_width = CORES * width
    head = q_weight.shape[2]
    features = q_weight.shape[1]
    toks = text_rows.shape[0] // MICRO
    own_slots = image_rows.shape[0]
    sent = vmem_call(
        lambda *refs: pack_kernel(ys, tps, *refs),
        jax.ShapeDtypeStruct((members, 2 * own_slots, chip_width), jnp.bfloat16),
        "pack",
        hbm=(image_target, image_rows, norm_gain, q_bias),
        scratch=[pltpu.SMEM(image_target.shape, jnp.int32)]
        + [pltpu.VMEM(a.shape, a.dtype) for a in (image_rows, norm_gain, q_bias)]
        + [pltpu.SemaphoreType.DMA((4,))],
    )
    sent, text_sent, q_sent, w_sent = lax.optimization_barrier(
        (sent, text_rows, q_weight[0], out_weight[0])
    )
    got = exchange(sent, plane)
    other_text = swap_cores(text_sent)
    other_q = swap_cores(q_sent)
    own_w = out_weight[0]
    other_w = swap_cores(w_sent)
    cosine, sine = tables(toks, head)
    got, other_text, other_q, other_w, cosine, sine = lax.optimization_barrier(
        (got, other_text, other_q, other_w, cosine, sine)
    )

    rows = jax.ShapeDtypeStruct((toks, chip_width), jnp.bfloat16)
    text_half = jax.ShapeDtypeStruct((toks, width), jnp.bfloat16)
    copies = jax.ShapeDtypeStruct((chip_count, toks, chip_width), jnp.bfloat16)
    contexts = jax.ShapeDtypeStruct((chip_count, toks, CORES * head), jnp.bfloat16)
    weights = jax.ShapeDtypeStruct((features, CORES * head), jnp.bfloat16)
    wide = (q_weight[0], other_q, kv_weight[0, :, 0])
    current, sent, query_w, keyval_w = vmem_call(
        lambda *refs: embed_kernel(own_slots, head, *refs),
        (rows, copies, weights, weights),
        "embed",
        got, other_text,
        hbm=(text_rows, *wide),
        scratch=[
            pltpu.VMEM(text_rows.shape, text_rows.dtype),
            pltpu.SemaphoreType.DMA,
            pltpu.SemaphoreType.DMA((LOAD_CHUNKS, 3)),
        ],
    )
    stored = ()
    for step in range(sections):
        if step > 0:
            order = [(i + step - 1) % sections for i in range(sections)]
            pairs = list(zip(order[::2], order[1::2]))
            route = pairs + [(b, a) for a, b in pairs]
            current = lax.ppermute(current, "section", route)
            sent = jnp.broadcast_to(current[None], copies.shape)
        gathered = exchange(sent, chips)
        if step == 0:
            context, query_w, keyval_w, gain, bias = vmem_call(
                lambda *refs: first_attend_kernel(tps, head, *refs),
                (
                    contexts,
                    weights,
                    weights,
                    jax.ShapeDtypeStruct((members, width), jnp.float32),
                    jax.ShapeDtypeStruct((1, 2 * CORES * head), jnp.float32),
                ),
                "attend_first",
                gathered, got, kv_bias[0], cosine, sine, query_w, keyval_w,
                hbm=wide,
                aliases={5: 1, 6: 2},
                scratch=[pltpu.SemaphoreType.DMA((LOAD_CHUNKS, 3))],
            )
        else:
            context = vmem_call(
                lambda *refs: attend_kernel(tps, head, step, *refs),
                contexts,
                "attend",
                gathered, gain, query_w, keyval_w, bias, cosine, sine,
            )
        last = step == sections - 1
        out = text_half if last else rows
        current, keep = vmem_call(
            lambda *refs: output_kernel(tps, step, last, *refs),
            (out, out),
            "output",
            exchange(context, chips), own_w, other_w, current, *stored,
        )
        stored = (keep,)
    joined = jax.ShapeDtypeStruct((MICRO * toks, width), jnp.bfloat16)
    return vmem_call(join_kernel, joined, "join", current, swap_cores(keep))[None]


def solution(mesh):
    sections, seqs, tps = (mesh.shape[name] for name in ("section", "seq", "tp"))
    fine = Mesh(
        mesh.devices.reshape(sections, seqs // CORES, CORES, tps), ("section", "y", "core", "tp")
    )
    seq = ("y", "core")
    in_specs = (
        P(None, (*seq, "tp")),
        P((*seq, "tp"), None),
        P((*seq, "tp")),
        P("section", (*seq, "tp")),
        P("section", None, (*seq, "tp")),
        P("section", (*seq, "tp")),
        P("section", None, "tp", None),
        P("section", "tp", None),
        P("section", None, (*seq, "tp")),
    )
    out_specs = P("section", None, (*seq, "tp"))
    return jax.shard_map(
        per_device, mesh=fine, in_specs=in_specs, out_specs=out_specs, check_vma=False
    )
```
